256 devices in a mesh: pts: 8 (over z_lo, core), coord: 32 (over y, z_hi, x).
Axes of the slice: x: 4, y: 4, z: 8 (z_hi: 2, z_lo: 4; z = z_hi * 4 + z_lo), core: 2. Of those that a mesh axis runs over, the one named last changes fastest.
Arguments:
- point_seed: int32 [512], P('pts'), may hold values from 0 to 16777215
- pert_seed: int32 [512, 16], P('pts'), may hold values from 0 to 16777215
- source_coef: float32 [100000], P('coord'), may hold values from -9 to 9
- w1: bfloat16 [1024, 100000], P(None, 'coord'), may hold values from -0.009765625 to 0.009765625
- b1: float32 [1024], replicated, may hold values from -3 to 3
- w2: bfloat16 [1024, 1024], replicated, may hold values from -0.1875 to 0.1875
- w3: bfloat16 [1024], replicated, may hold values from -0.1875 to 0.1875
Outputs:
- residual: float32 [512], P(('pts', 'coord'))
- grad_w1: bfloat16 [1024, 100000], P('pts', 'coord')
- grad_w2: float32 [1024, 1024], P('coord')
- grad_b1: float32 [1024], P('coord')
- grad_w3: float32 [1024], P('coord')
The draws below stay inside these ranges and needn't reach their ends.
All inputs are finite; a program needn't handle non-finite values.
Results may differ from the reference program's by a relative error of at most 0.023.
Values may be sent and summed in bfloat16 or wider, within the bound.
A program may use at most 128 MiB of HBM per device.

```python
import math
import jax
import jax.numpy as jnp
from jax import lax

D = 100000
H = 1024
K = 16
PTS_DEV = 64
POINTS = 512
N_PTS = 8


def draw_source_coef(key, part):
    position = jnp.arange(D, dtype=jnp.float32) / (D - 1)
    normal_part = jax.random.truncated_normal(key, -3.0, 3.0, (D,), jnp.float32)
    return normal_part * (1.0 + 2.0 * position)


def place_ends(drawn, own_key, least, high):
    spot = [jax.random.randint(jax.random.fold_in(own_key, axis), (), 0, length) for axis, length in enumerate(drawn.shape)]
    main_axis = drawn.shape.index(max(drawn.shape))
    next_to = spot[:main_axis] + [(spot[main_axis] + 1) % drawn.shape[main_axis]] + spot[main_axis + 1:]
    return drawn.at[tuple(spot)].set(least).at[tuple(next_to)].set(high)


def block_levels(rng, extent, cuts, smallest, largest):
    level, own = 1.0, jax.random.fold_in(rng, 6)
    for dim, blocks in cuts:
        heights = jnp.exp(jax.random.uniform(jax.random.fold_in(own, dim), (blocks,), jnp.float32, smallest / len(cuts), largest / len(cuts)))
        level = level * jnp.repeat(heights, extent[dim] // blocks).reshape([-1 if axis == dim else 1 for axis in range(len(extent))])
    return level


def scatter_about(own_key, extent, width, most, shards=(), kind=jnp.bfloat16):
    drawn = width * jax.random.normal(own_key, extent, jnp.float32)
    if shards:
        drawn = drawn * block_levels(own_key, extent, shards, -0.22, 0.18)
    return jnp.clip(drawn, -most, most).astype(kind)


def setup_inputs(seed: int = 0) -> dict:
    streams_of = jax.random.split(jax.random.key(seed), 8)
    point_seed = place_ends(jax.random.randint(streams_of[0], (POINTS,), 0, 16777216), jax.random.fold_in(streams_of[0], 1), 0, 16777215).astype(jnp.int32)
    pert_seed = place_ends(jax.random.randint(streams_of[1], (POINTS, K), 0, 16777216), jax.random.fold_in(streams_of[1], 1), 0, 16777215).astype(jnp.int32)
    source_coef = draw_source_coef(jax.random.fold_in(streams_of[7], 71), 0)
    w1 = scatter_about(streams_of[3], (H, D), (4 * D) ** -0.5, 0.009765625, ((1, 32),))
    b1 = scatter_about(streams_of[4], (H,), 0.5, 3.0, (), jnp.float32)
    w2 = scatter_about(streams_of[5], (H, H), H ** -0.5, 0.1875)
    w3 = scatter_about(streams_of[6], (H,), H ** -0.5, 0.1875)
    return dict(point_seed=point_seed, pert_seed=pert_seed, source_coef=source_coef, w1=w1, b1=b1, w2=w2, w3=w3)


hash_factor = 73244475
NOISE_SCALE = 2.0
READOUT = 0.0625

def shuffle_bits(packed_bits):
    return packed_bits ^ lax.shift_right_logical(packed_bits, jnp.full_like(packed_bits, 16))

def mix_bits(packed_bits):
    packed_bits = shuffle_bits(packed_bits)
    packed_bits = shuffle_bits(packed_bits * hash_factor)
    return shuffle_bits(packed_bits * hash_factor)

def to_unit(packed_bits):
    return ((packed_bits & 8388607).astype(jnp.float32) + 0.5) * (1.0 / 8388608.0)

def column_keys(columns):
    return (mix_bits(columns * 4), mix_bits(columns * 4 + 1), mix_bits(columns * 4 + 2))

def perturbed_rows(point_seeds, pert_seeds, column_hash, coef_part):
    key_zero, key_one, key_two = column_hash
    count_points, count_samples = pert_seeds.shape
    uniform_point = to_unit(mix_bits(key_two[None, :] ^ point_seeds[:, None]))
    coords = 2.0 * uniform_point - 1.0
    uniform_zero = to_unit(mix_bits(key_zero[None, None, :] ^ pert_seeds[:, :, None]))
    uniform_one = to_unit(mix_bits(key_one[None, None, :] ^ pert_seeds[:, :, None]))
    noise_draw = jnp.sqrt(-2.0 * jnp.log(uniform_zero)) * jnp.cos(2.0 * jnp.pi * uniform_one)
    shifted = (coords[:, None, :] + NOISE_SCALE * noise_draw).astype(jnp.bfloat16)
    shifted = shifted.reshape(count_points * count_samples, coords.shape[1])
    squares = lax.optimization_barrier(jnp.sum(noise_draw * noise_draw, axis=2)).reshape(count_points * count_samples)
    source = lax.optimization_barrier(jnp.sum(coef_part[None, :] * jnp.sin(jnp.pi * coords), axis=1)) / math.sqrt(D)
    return (shifted, squares, source)

def hidden_pass(pre_first, squares, source, w2, w3, count_samples):
    hidden_one = jnp.tanh(pre_first).astype(jnp.bfloat16)
    pre_second = lax.dot_general(hidden_one, w2, (((1,), (1,)), ((), ())), preferred_element_type=jnp.float32)
    hidden_two = jnp.tanh(pre_second).astype(jnp.bfloat16)
    values_out = READOUT * jnp.dot(hidden_two, w3, preferred_element_type=jnp.float32)
    stein_weight = (squares - D) / (NOISE_SCALE * NOISE_SCALE * count_samples)
    per_point = (stein_weight * values_out).reshape(-1, count_samples)
    residual = lax.optimization_barrier(jnp.sum(per_point, axis=1)) - source
    grad_values = (residual[:, None] * stein_weight.reshape(-1, count_samples)).reshape(-1)
    two_float = hidden_two.astype(jnp.float32)
    grad_readout = READOUT * lax.optimization_barrier(jnp.sum(grad_values[:, None] * two_float, axis=0))
    grad_pre_two = (READOUT * grad_values[:, None] * w3.astype(jnp.float32)[None, :] * (1.0 - two_float * two_float)).astype(jnp.bfloat16)
    grad_second = lax.dot_general(grad_pre_two, hidden_one, (((0,), (0,)), ((), ())), preferred_element_type=jnp.float32)
    grad_hidden = jnp.dot(grad_pre_two, w2, preferred_element_type=jnp.float32)
    one_float = hidden_one.astype(jnp.float32)
    grad_pre_one = (grad_hidden * (1.0 - one_float * one_float)).astype(jnp.bfloat16)
    grad_bias = lax.optimization_barrier(jnp.sum(grad_pre_one.astype(jnp.float32), axis=0))
    return (residual, grad_pre_one, grad_second, grad_bias, grad_readout)

def reference(point_seed, pert_seed, source_coef, w1, b1, w2, w3):
    column_hash = column_keys(jnp.arange(D, dtype=jnp.int32))
    block_count = POINTS // 8
    point_blocks = point_seed.reshape(block_count, 8)
    pert_blocks = pert_seed.reshape(block_count, 8, K)

    def forward_block(block_args):
        shifted, squares, source = perturbed_rows(block_args[0], block_args[1], column_hash, source_coef)
        pre_block = lax.dot_general(shifted, w1, (((1,), (1,)), ((), ())), preferred_element_type=jnp.float32)
        return (pre_block, squares, source)
    pre_blocks, square_blocks, source_blocks = lax.map(forward_block, (point_blocks, pert_blocks))
    pre_first = pre_blocks.reshape(POINTS * K, H) + b1[None, :]
    residual, grad_pre_one, grad_second, grad_bias, grad_readout = hidden_pass(pre_first, square_blocks.reshape(POINTS * K), source_blocks.reshape(POINTS), w2, w3, K)
    inner_count = PTS_DEV // 8
    grad_groups = grad_pre_one.reshape(N_PTS, inner_count, 8 * K, H)
    point_groups = point_seed.reshape(N_PTS, inner_count, 8)
    pert_groups = pert_seed.reshape(N_PTS, inner_count, 8, K)

    def block_term(accum, inner_args):
        shifted = perturbed_rows(inner_args[1], inner_args[2], column_hash, source_coef)[0]
        contrib = lax.dot_general(inner_args[0], shifted, (((0,), (0,)), ((), ())), preferred_element_type=jnp.float32)
        return (accum + contrib, None)

    def group_term(running, group_args):
        group_sum, _ = lax.scan(block_term, jnp.zeros((H, D), jnp.float32), group_args)
        rounded = lax.optimization_barrier(group_sum.astype(jnp.bfloat16)).astype(jnp.float32)
        return (running + rounded, None)
    summed, _ = lax.scan(group_term, jnp.zeros((H, D), jnp.float32), (grad_groups, point_groups, pert_groups))
    return (residual, summed.astype(jnp.bfloat16), grad_second, grad_bias, grad_readout)
```

```python
import math

import jax
import jax.numpy as jnp
from jax import lax
from jax.experimental import pallas as pl
from jax.experimental.pallas import tpu as pltpu
from jax.sharding import PartitionSpec as P

D = 100000
HASH = 73244475
MESH = pl.DeviceIdType.MESH
F32, BF16, I32 = jnp.float32, jnp.bfloat16, jnp.int32
SINE = (1.5707962900223675, -0.6459633598658464, 0.07968848054018324, -0.004672227923047835, 0.00015082056445751214)
LOW = 8388607
UNIT = 1.0 / 8388608.0

XY = 16
ROWS = 64
HID = 1024
WIDTH = 3125
LANES = 3200
SUB = 640
NSUB = LANES // SUB
KC = 256
WIDE = HID + 128


def shuffle_bits(v):
    return v ^ lax.shift_right_logical(v, jnp.full_like(v, 16))


def rounds(v):
    v = shuffle_bits(v * HASH)
    return shuffle_bits(v * HASH)


def sine(y, scale):
    t = y * y
    acc = t * (SINE[4] * scale) + (SINE[3] * scale)
    for c in (SINE[2], SINE[1], SINE[0]):
        acc = acc * t + (c * scale)
    return acc * y


def kernel(
    seed_ref, pseed_ref, coef_ref, w1_ref, w1t_ref, b1_ref, w2_ref, w3_ref,
    res_ref, grad_ref, g2_ref,
    w1s, w2s, zs, xs, hs, sqs, srcs, acc,
    psend, precv, ssend, srecv, zsend, zrecv, tsend, trecv,
    h1s, h2s, d2s, dbuf, dall, dt, own, bsend, brecv, tmp, lsend, lrecv, rsend, rrecv,
    gbuf, grecv, gtot, hsend, hrecv, csend, crecv, fsend, frecv,
    load_sem, p_ss, p_rs, s_ss, s_rs, z_ss, z_rs, a_ss, a_rs, b_ss, b_rs,
    l_ss, l_rs, r_ss, r_rs, g_ss, g_rs, h_ss, h_rs, c_ss, c_rs,
):
    pts, coord = lax.axis_index("pts"), lax.axis_index("coord")
    zlo, core = pts // 2, pts % 2
    mx, zh, my = coord % 4, (coord // 4) % 2, coord // 8
    me = my * 4 + mx

    def plane(t):
        return (pts, (t // 4) * 8 + zh * 4 + t % 4)

    zpeer = (pts, coord + 4 - 8 * zh)
    sibling = (pts + 1 - 2 * core, coord)

    def chip(z):
        return (z * 2 + core, coord)

    def remote(src, dst, ss, rs, device):
        return pltpu.make_async_remote_copy(src, dst, ss, rs, device_id=device, device_id_type=MESH)

    def each(lo, hi, body):
        def run(i, c):
            body(i)
            return c

        lax.fori_loop(lo, hi, run, 0)

    loads = [
        pltpu.make_async_copy(w1_ref.at[pl.ds(0, 3072)], w1s.at[pl.ds(0, 3072)], load_sem.at[0]),
        pltpu.make_async_copy(w1t_ref, w1s.at[pl.ds(3072, 128)], load_sem.at[1]),
        pltpu.make_async_copy(w2_ref, w2s, load_sem.at[2]),
    ]
    for c in loads:
        c.start()
    barrier = pltpu.get_barrier_semaphore()

    def greet(device):
        pl.semaphore_signal(barrier, inc=1, device_id=device, device_id_type=MESH)

    each(1, XY, lambda p: greet(plane((me + p) % XY)))
    greet(zpeer)
    greet(sibling)
    for p in (1, 2, 3):
        greet(chip((zlo + p) % 4))

    srcs[...] = jnp.zeros_like(srcs)
    sqs[...] = jnp.zeros_like(sqs)
    lane8 = lax.broadcasted_iota(I32, (8, 128), 1)
    row8 = lax.broadcasted_iota(I32, (8, 128), 0)

    def points(k):
        at = pl.ds(pl.multiple_of(k * 128, 128), 128)
        col = (coord * WIDTH + k * 128 + lane8) * 4
        for n in range(3):
            h = rounds(shuffle_bits(col + n))
            if n < 2:
                hs[n, :, at] = shuffle_bits(h)
        h = shuffle_bits(h)
        coef = jnp.broadcast_to(coef_ref[:, at], (8, 128))
        for g in range(8):
            v = rounds(h ^ pseed_ref[8 * g:8 * g + 8, :])
            t = (v & LOW).astype(F32) + (0.5 - 4194304.0)
            x = t * (2.0 * UNIT)
            y = t * (4.0 * UNIT)
            fold = 1.0 - jnp.abs(jnp.abs(y) - 1.0)
            s = coef * sine(jnp.where(y < 0, -fold, fold), 1.0)
            for i in range(2):
                xs[g * 2 + i, 0:4, at] = x[4 * i:4 * i + 4]
                srcs[g * 2 + i, 0:4, :] += s[4 * i:4 * i + 4]

    each(0, LANES // 128, points)

    def target(s, i):
        if i == 0:
            dx, dy = 2 * (1 - s // 2), 2 * (1 - s % 2)
        elif i == 1:
            dx, dy = 1, 3 - s
        elif i == 2:
            dx, dy = 3, (s + 1) % 4
        else:
            dx, dy = 2 * (1 - s // 2), 3 - 2 * (s % 2)
        return ((my + dy) % 4) * 4 + (mx + dx) % 4

    def noise(ts, k, width, mask):
        for l in range(width // 128):
            at = pl.ds(pl.multiple_of(k * KC + l * 128, 128), 128)
            h0, h1 = hs[0, :, at], hs[1, :, at]
            h0 = jnp.concatenate([h0, h0], axis=0)
            h1 = jnp.concatenate([h1, h1], axis=0)
            for t in ts:
                for p in range(4):
                    here = pl.ds(p * 16, 16)
                    seed = seed_ref[t, here, :]
                    u0 = ((rounds(h0 ^ seed) & LOW).astype(F32) + 0.5) * UNIT
                    r = jnp.sqrt(-2.0 * jnp.log(u0))
                    a = (rounds(h1 ^ seed) & LOW).astype(F32) + (0.5 - 4194304.0)
                    y = (jnp.abs(a) - 2097152.0) * (4.0 * UNIT)
                    e = r * sine(y, 2.0)
                    x = jnp.broadcast_to(xs[t, p:p + 1, at], (16, 128))
                    z = x + e
                    q = e * e
                    if mask is not None:
                        z = jnp.where(mask, z, 0.0)
                        q = jnp.where(mask, q, 0.0)
                    zs[t, here, at] = z.astype(BF16)
                    sqs[t, here, :] += q

    def first_layer(ts, k, width):
        at = pl.ds(pl.multiple_of(k * KC, 128), width)
        left = jnp.concatenate([zs[t, :, at] for t in ts], axis=0)
        acc[...] += jnp.dot(left, w1s[at, :], preferred_element_type=F32)

    eye = jnp.where(
        lax.broadcasted_iota(I32, (ROWS, 128), 0) == lax.broadcasted_iota(I32, (ROWS, 128), 1), 1.0, 0.0
    )
    tail_mask = lax.broadcasted_iota(I32, (16, 128), 1) < WIDTH - 3072

    def stats_of(t):
        sq = jnp.sum(sqs[t], axis=1, keepdims=True)
        row_sq = jnp.sum(eye * sq, axis=0, keepdims=True)
        src = jnp.sum(srcs[t], axis=1, keepdims=True)
        row_src = jnp.sum(jnp.where(lane8 // 16 == row8, src, 0.0), axis=0, keepdims=True)
        return jnp.where(row8 == 0, row_sq, jnp.where(row8 == 1, row_src, 0.0))

    def partial_copy(t, slot):
        return remote(psend.at[t], precv.at[slot], p_ss.at[t], p_rs.at[slot], plane(t))

    def stat_copy(t, slot):
        return remote(ssend.at[t], srecv.at[slot], s_ss.at[t], s_rs.at[slot], plane(t))

    loads[0].wait()
    loads[1].wait()

    def step(s):
        ts = [target(s, i) for i in range(4)]
        acc[...] = jnp.zeros_like(acc)
        noise(ts, 0, KC, None)

        def inner(k):
            first_layer(ts, k - 1, KC)
            noise(ts, k, KC, None)

        each(1, 12, inner)
        first_layer(ts, 11, KC)
        noise(ts, 12, 128, tail_mask)
        first_layer(ts, 12, 128)

        @pl.when(s == 0)
        def _():
            pl.semaphore_wait(barrier, XY - 1 + 5)

        for i, t in enumerate(ts):
            value = acc[i * ROWS:(i + 1) * ROWS, :].astype(BF16)
            tile = stats_of(t)
            if i > 0:
                psend[t] = value
                ssend[t] = tile
                partial_copy(t, me).start()
                stat_copy(t, me).start()
                continue

            @pl.when(s < 3)
            def _():
                psend[t] = value
                ssend[t] = tile
                partial_copy(t, me).start()
                stat_copy(t, me).start()

            @pl.when(s == 3)
            def _():
                precv[me] = value
                srecv[me] = tile

    each(0, 4, step)

    def arrived(p):
        slot = (me + p) % XY
        partial_copy(slot, slot).wait_recv()
        stat_copy(slot, slot).wait_recv()

    each(1, XY, arrived)

    def plane_sum(r):
        at = pl.ds(pl.multiple_of(r * 16, 16), 16)
        tot = precv[0, at, :].astype(F32)
        for n in range(1, XY):
            tot += precv[n, at, :].astype(F32)
        zsend[at, :] = tot.astype(BF16)

    each(0, ROWS // 16, plane_sum)
    tot = srecv[0]
    for n in range(1, XY):
        tot += srecv[n]
    tsend[...] = tot
    z_copy = remote(zsend, zrecv, z_ss.at[0], z_rs.at[0], zpeer)
    t_copy = remote(tsend, trecv, z_ss.at[1], z_rs.at[1], zpeer)
    z_copy.start()
    t_copy.start()
    loads[2].wait()
    z_copy.wait_recv()
    t_copy.wait_recv()

    pre = (zsend[...].astype(F32) + zrecv[...].astype(F32)) + b1_ref[...]
    h1 = jnp.tanh(pre).astype(BF16)
    h1s[...] = h1
    two = jnp.tanh(
        lax.dot_general(h1, w2s[...], (((1,), (1,)), ((), ())), preferred_element_type=F32)
    ).astype(BF16)
    stat = tsend[...] + trecv[...]
    sq = jnp.sum(eye * stat[0:1, :], axis=1, keepdims=True) * 0.25
    src = jnp.sum(eye * stat[1:2, :], axis=1, keepdims=True) / math.sqrt(D)
    two_float = two.astype(F32)
    w3 = w3_ref[...]
    value = 0.0625 * jnp.sum(two_float * w3, axis=1, keepdims=True)
    stein = (sq - D) / 64.0
    prod = jnp.broadcast_to(stein * value, (ROWS, 128)).reshape(4, 16, 128)
    residual = jnp.broadcast_to(jnp.sum(prod, axis=1, keepdims=True), (4, 16, 128)).reshape(ROWS, 128) - src
    res_ref[...] = jnp.zeros_like(res_ref)
    for n in range(2):
        @pl.when(zh == n)
        def _():
            res_ref[0:1, :] = residual[32 * n:32 * n + 1, :]
            res_ref[1:2, :] = residual[32 * n + 16:32 * n + 17, :]

    dval = residual * stein
    dpre2 = (0.0625 * dval[:, 0:1] * w3 * (1.0 - two_float * two_float)).astype(BF16)
    back = jnp.dot(dpre2, w2s[...], preferred_element_type=F32)
    one_float = h1.astype(F32)
    dpre1 = (back * (1.0 - one_float * one_float)).astype(BF16)
    for j in range(4):
        part = dpre1[:, 256 * j:256 * j + 256]
        dbuf[j] = part
        dall[j, me] = part
        h2s[j] = two[:, 256 * j:256 * j + 256]
        d2s[j] = dpre2[:, 256 * j:256 * j + 256]

    def gather_copy(j, t, slot):
        return remote(dbuf.at[j], dall.at[j, slot], a_ss.at[j * XY + t], a_rs.at[j * XY + slot], plane(t))

    for j in (3, 0, 2, 1):
        each(1, XY, lambda p, j=j: gather_copy(j, (me + p) % XY, me).start())

    lane64 = lax.broadcasted_iota(I32, (ROWS, 128), 1)
    high = dval.astype(BF16)
    low = (dval - high.astype(F32)).astype(BF16)
    zero = jnp.zeros_like(dval)
    pick0 = jnp.where(lane64 == 0, 1.0, zero).astype(BF16)
    pick1 = jnp.where(lane64 == 1, high.astype(F32), jnp.where(lane64 == 2, low.astype(F32), zero)).astype(BF16)
    rows_of = (((0,), (0,)), ((), ()))
    half = pl.ds(pl.multiple_of(zh * 128, 128), 128)
    for j in range(4):
        main = lax.dot_general(d2s[j, :, half], h1, rows_of, preferred_element_type=F32)
        more = lax.dot_general(dbuf[j, :, half], pick0, rows_of, preferred_element_type=F32)
        more += lax.dot_general(h2s[j, :, half], pick1, rows_of, preferred_element_type=F32)
        gbuf[j, :, 0:HID] = main.astype(BF16)
        gbuf[j, :, HID:WIDE] = more.astype(BF16)
    grecv[me] = gbuf[my, pl.ds(pl.multiple_of(mx * 32, 32), 32), :]

    def small_copy(t, slot):
        mine = gbuf.at[t // 4, pl.ds(pl.multiple_of((t % 4) * 32, 32), 32)]
        return remote(mine, grecv.at[slot], g_ss.at[t], g_rs.at[slot], plane(t))

    each(1, XY, lambda p: small_copy((me + p) % XY, me).start())

    def core_copy(n):
        return remote(bsend.at[n], brecv.at[n], b_ss.at[n], b_rs.at[n], sibling)

    def chunk(j):
        def there(p):
            slot = (me + p) % XY
            gather_copy(j, slot, slot).wait_recv()

        each(1, XY, there)
        for n, c in enumerate((1 - core, core)):
            block = dall[j, :, :, pl.ds(pl.multiple_of(c * 128, 128), 128)].reshape(XY * ROWS, 128)
            dt[128 * n:128 * n + 128, :] = jnp.transpose(block)

        def sub(b):
            at = pl.ds(pl.multiple_of(b * SUB, 128), SUB)
            right = zs[:, :, at].reshape(XY * ROWS, SUB)
            part = jnp.dot(dt[...], right, preferred_element_type=F32)
            n = j * NSUB + b
            bsend[n] = part[0:128].astype(BF16)
            core_copy(n).start()
            own[n] = part[128:256]

        each(0, NSUB, sub)

    def right_copy(n):
        return remote(lsend.at[n], lrecv.at[n], l_ss.at[n], l_rs.at[n], chip(zlo + 1))

    def left_copy(n):
        return remote(rsend.at[n], rrecv.at[n], r_ss.at[n], r_rs.at[n], chip(zlo - 1))

    def chip_sum(n):
        core_copy(n).wait_recv()
        return own[n] + brecv[n].astype(F32)

    def go_right(t, b):
        n = t * NSUB + b
        tmp[...] = chip_sum((3 - t) * NSUB + b)

        @pl.when(zlo > 0)
        def _():
            remote(lsend.at[n], lrecv.at[n], l_ss.at[n], l_rs.at[n], chip(zlo - 1)).wait_recv()
            tmp[...] += lrecv[n].astype(F32)

        lsend[n] = tmp[...].astype(BF16)
        right_copy(n).start()

    def go_left(t, b):
        n = t * NSUB + b
        tmp[...] = chip_sum(n)

        @pl.when(zlo < 3)
        def _():
            remote(rsend.at[n], rrecv.at[n], r_ss.at[n], r_rs.at[n], chip(zlo + 1)).wait_recv()
            tmp[...] += rrecv[n].astype(F32)

        rsend[n] = tmp[...].astype(BF16)
        left_copy(n).start()

    each(0, 2, lambda q: chunk(3 - 3 * q))

    @pl.when(zlo == 0)
    def _():
        each(0, NSUB, lambda b: go_right(0, b))

    @pl.when(zlo == 3)
    def _():
        each(0, NSUB, lambda b: go_left(0, b))

    each(0, 2, lambda q: chunk(2 - q))

    def small_there(p):
        slot = (me + p) % XY
        small_copy(slot, slot).wait_recv()

    each(1, XY, small_there)
    for r in range(2):
        at = slice(16 * r, 16 * r + 16)
        tot = grecv[0, at, :].astype(F32)
        for n in range(1, XY):
            tot += grecv[n, at, :].astype(F32)
        gtot[at, :] = tot
    theirs = pl.ds(pl.multiple_of(16 * (1 - core), 16), 16)
    mine = pl.ds(pl.multiple_of(16 * core, 16), 16)
    hsend[...] = gtot[theirs, :].astype(BF16)
    h_copy = remote(hsend, hrecv, h_ss.at[0], h_rs.at[0], sibling)
    h_copy.start()

    def line(t):
        def both(b):
            @pl.when((3 - t > zlo) & (zlo > (0 if t == 0 else -1)))
            def _():
                go_right(t, b)

            @pl.when((t < zlo) & (zlo < (3 if t == 0 else 4)))
            def _():
                go_left(t, b)

        each(0, NSUB, both)

    def across(z, slot):
        return remote(csend, crecv.at[slot], c_ss.at[z], c_rs.at[slot], chip(z))

    line(0)
    h_copy.wait_recv()
    total = (gtot[mine, :] + hrecv[...].astype(F32)).astype(BF16)
    csend[...] = total
    crecv[zlo] = total
    for p in (1, 2, 3):
        across((zlo + p) % 4, zlo).start()
    line(1)
    for p in (1, 2, 3):
        across((zlo + p) % 4, (zlo + p) % 4).wait_recv()
    total = crecv[0].astype(F32)
    for n in range(1, 4):
        total += crecv[n].astype(F32)
    fsend[...] = total
    g2_ref[mine, :] = total
    f_copy = remote(fsend, frecv, h_ss.at[1], h_rs.at[1], sibling)
    f_copy.start()
    line(2)
    f_copy.wait_recv()
    g2_ref[theirs, :] = frecv[...]

    def finish(b):
        tmp[...] = chip_sum(zlo * NSUB + b)

        @pl.when(zlo > 0)
        def _():
            n = (3 - zlo) * NSUB + b
            remote(lsend.at[n], lrecv.at[n], l_ss.at[n], l_rs.at[n], chip(zlo - 1)).wait_recv()
            tmp[...] += lrecv[n].astype(F32)

        @pl.when(zlo < 3)
        def _():
            n = zlo * NSUB + b
            remote(rsend.at[n], rrecv.at[n], r_ss.at[n], r_rs.at[n], chip(zlo + 1)).wait_recv()
            tmp[...] += rrecv[n].astype(F32)

        grad_ref[:, pl.ds(pl.multiple_of(b * SUB, 128), SUB)] = tmp[...].astype(BF16)

    each(0, NSUB, finish)

    def left_plane(p):
        t = (me + p) % XY
        partial_copy(t, me).wait_send()
        stat_copy(t, me).wait_send()
        small_copy(t, me).wait_send()
        for j in range(4):
            gather_copy(j, t, me).wait_send()

    each(1, XY, left_plane)
    z_copy.wait_send()
    t_copy.wait_send()
    h_copy.wait_send()
    f_copy.wait_send()
    for p in (1, 2, 3):
        across((zlo + p) % 4, zlo).wait_send()
    each(0, 4 * NSUB, lambda n: core_copy(n).wait_send())
    each(0, (3 - zlo) * NSUB, lambda n: right_copy(n).wait_send())
    each(0, zlo * NSUB, lambda n: left_copy(n).wait_send())


def shards(point_seed, pert_seed, source_coef, w1, b1, w2, w3):
    seeds = shuffle_bits(pert_seed).reshape(4, 2, 4, 2, 16).transpose(0, 2, 1, 3, 4)
    seeds = jnp.broadcast_to(seeds.reshape(XY, ROWS)[:, :, None], (XY, ROWS, 128))
    pseeds = shuffle_bits(point_seed).reshape(4, 2, 4, 2).transpose(0, 2, 1, 3)
    pseeds = jnp.broadcast_to(pseeds.reshape(64)[:, None], (64, 128))
    coef = jnp.pad(source_coef, (0, LANES - WIDTH)).reshape(1, LANES)
    w1t = w1.T
    tail = jnp.pad(w1t[3072:], ((0, LANES - WIDTH), (0, 0)))
    vmem = pl.BlockSpec(memory_space=pltpu.VMEM)
    anyw = pl.BlockSpec(memory_space=pl.ANY)
    dma = lambda n: pltpu.SemaphoreType.DMA((n,))
    v = pltpu.VMEM
    n15, n20 = 3 * NSUB, 4 * NSUB
    residual, grad, small = pl.pallas_call(
        kernel,
        name="pinn_step",
        out_shape=(
            jax.ShapeDtypeStruct((8, 128), F32),
            jax.ShapeDtypeStruct((128, LANES), BF16),
            jax.ShapeDtypeStruct((32, WIDE), F32),
        ),
        in_specs=[vmem, vmem, vmem, anyw, anyw, vmem, anyw, vmem],
        out_specs=(vmem, vmem, vmem),
        scratch_shapes=[
            v((LANES, HID), BF16), v((HID, HID), BF16), v((XY, ROWS, LANES), BF16),
            v((XY, 8, LANES), F32), v((2, 8, LANES), I32), v((XY, ROWS, 128), F32), v((XY, 8, 128), F32),
            v((256, HID), F32),
            v((XY, ROWS, HID), BF16), v((XY, ROWS, HID), BF16), v((XY, 8, 128), F32), v((XY, 8, 128), F32),
            v((ROWS, HID), BF16), v((ROWS, HID), BF16), v((8, 128), F32), v((8, 128), F32),
            v((ROWS, HID), BF16), v((4, ROWS, 256), BF16), v((4, ROWS, 256), BF16), v((4, ROWS, 256), BF16),
            v((4, XY, ROWS, 256), BF16), v((256, XY * ROWS), BF16),
            v((n20, 128, SUB), F32), v((n20, 128, SUB), BF16), v((n20, 128, SUB), BF16), v((128, SUB), F32),
            v((n15, 128, SUB), BF16), v((n15, 128, SUB), BF16), v((n15, 128, SUB), BF16), v((n15, 128, SUB), BF16),
            v((4, 128, WIDE), BF16), v((XY, 32, WIDE), BF16), v((32, WIDE), F32),
            v((16, WIDE), BF16), v((16, WIDE), BF16), v((16, WIDE), BF16), v((4, 16, WIDE), BF16),
            v((16, WIDE), F32), v((16, WIDE), F32),
            dma(3), dma(XY), dma(XY), dma(XY), dma(XY), dma(2), dma(2), dma(4 * XY), dma(4 * XY), dma(n20), dma(n20),
            dma(n15), dma(n15), dma(n15), dma(n15), dma(XY), dma(XY), dma(2), dma(2), dma(4), dma(4),
        ],
        compiler_params=pltpu.CompilerParams(
            collective_id=0, has_side_effects=True, vmem_limit_bytes=66_000_000
        ),
    )(seeds, pseeds, coef, w1t, tail, b1.reshape(1, HID), w2, w3.astype(F32).reshape(1, HID))
    return (
        residual[0:2, 0],
        grad[:, :WIDTH],
        small[:, :HID],
        small[:, HID],
        0.0625 * (small[:, HID + 1] + small[:, HID + 2]),
    )


def solution(mesh):
    return jax.shard_map(
        shards,
        mesh=mesh,
        in_specs=(P("pts"), P("pts", None), P("coord"), P(None, "coord"), P(), P(), P()),
        out_specs=(
            P(("pts", "coord")),
            P("pts", "coord"),
            P("coord", None),
            P("coord"),
            P("coord"),
        ),
        check_vma=False,
    )
```

```python
import math

import jax
import jax.numpy as jnp
from jax import lax
from jax.experimental import pallas as pl
from jax.experimental.pallas import tpu as pltpu
from jax.sharding import PartitionSpec as P

D = 100000
HASH = 73244475
MESH = pl.DeviceIdType.MESH
F32, BF16, I32 = jnp.float32, jnp.bfloat16, jnp.int32
SINE = (1.5707962900223675, -0.6459633598658464, 0.07968848054018324, -0.004672227923047835, 0.00015082056445751214)
LOW = 8388607
UNIT = 1.0 / 8388608.0

XY = 16
ROWS = 64
HID = 1024
WIDTH = 3125
LANES = 3200
SUB = 640
NSUB = LANES // SUB
LAG = 2
KC = 256
WIDE = HID + 128

TREE = (
    ((2, 2), (1, 0)), ((2, 1), (0, 1)), ((2, -1), (-1, 0)), ((-1, 2), (0, -1)),
    ((1, 2), (0, 1)), ((2, 0), (1, 0)), ((0, 2), (0, -1)), ((-1, -1), (-1, 0)),
    ((1, 1), (1, 0)), ((-1, 1), (0, 1)), ((1, -1), (0, -1)), ((0, -1), (0, -1)),
    ((1, 0), (1, 0)), ((-1, 0), (-1, 0)), ((0, 1), (0, 1)), ((0, 0), None),
)


def lands(n):
    (a, b), move = TREE[n]
    if move is None:
        return None
    return tuple((v + 1) % 4 - 1 for v in (a - move[0], b - move[1]))


CHILDREN = [[m for m in range(XY) if lands(m) == TREE[n][0]] for n in range(XY)]
assert all(m // 4 < n // 4 for n in range(XY - 1) for m in CHILDREN[n])


def shuffle_bits(v):
    return v ^ lax.shift_right_logical(v, jnp.full_like(v, 16))


def rounds(v):
    v = shuffle_bits(v * HASH)
    return shuffle_bits(v * HASH)


def sine(y, scale):
    t = y * y
    acc = t * (SINE[4] * scale) + (SINE[3] * scale)
    for c in (SINE[2], SINE[1], SINE[0]):
        acc = acc * t + (c * scale)
    return acc * y


def kernel(
    pert_ref, point_ref, coef_ref, w1_ref, w1t_ref, b1_ref, w2_ref, w3_ref,
    res_ref, grad_ref, g2_ref,
    seed_ref, pseed_ref, w1s, w2s, zs, xs, hs, sqs, srcs, acc,
    psend, precv, ssend, srecv, zsend, zrecv, tsend, trecv,
    h1s, h2s, d2s, dbuf, dall, dt, own, bsend, brecv, tmp, lsend, lrecv, rsend, rrecv,
    gbuf, grecv, gtot, hsend, hrecv, csend, crecv, fsend, frecv,
    load_sem, p_ss, p_rs, s_ss, s_rs, z_ss, z_rs, a_ss, a_rs, b_ss, b_rs,
    l_ss, l_rs, r_ss, r_rs, g_ss, g_rs, h_ss, h_rs, c_ss, c_rs,
):
    pts, coord = lax.axis_index("pts"), lax.axis_index("coord")
    zlo, core = pts // 2, pts % 2
    mx, zh, my = coord % 4, (coord // 4) % 2, coord // 8
    me = my * 4 + mx

    def plane(t):
        return (pts, (t // 4) * 8 + zh * 4 + t % 4)

    zpeer = (pts, coord + 4 - 8 * zh)
    sibling = (pts + 1 - 2 * core, coord)

    def chip(z):
        return (z * 2 + core, coord)

    def remote(src, dst, ss, rs, device):
        return pltpu.make_async_remote_copy(src, dst, ss, rs, device_id=device, device_id_type=MESH)

    def each(lo, hi, body):
        def run(i, c):
            body(i)
            return c

        lax.fori_loop(lo, hi, run, 0)

    loads = [
        pltpu.make_async_copy(w1_ref.at[pl.ds(0, 3072)], w1s.at[pl.ds(0, 3072)], load_sem.at[0]),
        pltpu.make_async_copy(w1t_ref, w1s.at[pl.ds(3072, 128)], load_sem.at[1]),
        pltpu.make_async_copy(w2_ref, w2s, load_sem.at[2]),
    ]
    for c in loads:
        c.start()
    barrier = pltpu.get_barrier_semaphore()

    def greet(device):
        pl.semaphore_signal(barrier, inc=1, device_id=device, device_id_type=MESH)

    each(1, XY, lambda p: greet(plane((me + p) % XY)))
    greet(zpeer)
    greet(sibling)
    for p in (1, 2, 3):
        greet(chip((zlo + p) % 4))

    for n in range(64):
        pos = ((n // 16) * 4 + (n // 2) % 4, ((n // 8) % 2) * 2 + n % 2)
        seed = jnp.broadcast_to(pert_ref[:, n:n + 1], (16, 128))
        seed_ref[pos[0], 16 * pos[1]:16 * pos[1] + 16, :] = shuffle_bits(seed)
    r64 = lax.broadcasted_iota(I32, (64, 64), 0)
    place = (((r64 // 16) * 2 + (r64 // 2) % 2) * 4 + (r64 // 4) % 4) * 2 + r64 % 2
    spread = jnp.where(place == lax.broadcasted_iota(I32, (64, 64), 1), point_ref[...].astype(F32), 0.0)
    spread = jnp.sum(spread, axis=1, keepdims=True).astype(I32)
    pseed_ref[...] = shuffle_bits(jnp.broadcast_to(spread, (64, 128)))

    srcs[...] = jnp.zeros_like(srcs)
    sqs[...] = jnp.zeros_like(sqs)
    lane8 = lax.broadcasted_iota(I32, (8, 128), 1)
    row8 = lax.broadcasted_iota(I32, (8, 128), 0)

    def points(k):
        at = pl.ds(pl.multiple_of(k * 128, 128), 128)
        col = (coord * WIDTH + k * 128 + lane8) * 4
        for n in range(3):
            h = rounds(shuffle_bits(col + n))
            if n < 2:
                hs[n, :, at] = shuffle_bits(h)
        h = shuffle_bits(h)
        coef = jnp.broadcast_to(coef_ref[:, at], (8, 128))
        for g in range(8):
            v = rounds(h ^ pseed_ref[8 * g:8 * g + 8, :])
            t = (v & LOW).astype(F32) + (0.5 - 4194304.0)
            x = t * (2.0 * UNIT)
            y = t * (4.0 * UNIT)
            fold = 1.0 - jnp.abs(jnp.abs(y) - 1.0)
            s = coef * sine(jnp.where(y < 0, -fold, fold), 1.0)
            for i in range(2):
                xs[g * 2 + i, 0:4, at] = x[4 * i:4 * i + 4]
                srcs[g * 2 + i, 0:4, :] += s[4 * i:4 * i + 4]

    each(0, LANES // 128, points)

    def noise(ts, k, width, mask):
        for l in range(width // 128):
            at = pl.ds(pl.multiple_of(k * KC + l * 128, 128), 128)
            h0, h1 = hs[0, :, at], hs[1, :, at]
            h0 = jnp.concatenate([h0, h0], axis=0)
            h1 = jnp.concatenate([h1, h1], axis=0)
            for t in ts:
                for p in range(4):
                    here = pl.ds(p * 16, 16)
                    seed = seed_ref[t, here, :]
                    u0 = ((rounds(h0 ^ seed) & LOW).astype(F32) + 0.5) * UNIT
                    r = jnp.sqrt(-2.0 * jnp.log(u0))
                    a = (rounds(h1 ^ seed) & LOW).astype(F32) + (0.5 - 4194304.0)
                    y = (jnp.abs(a) - 2097152.0) * (4.0 * UNIT)
                    e = r * sine(y, 2.0)
                    x = jnp.broadcast_to(xs[t, p:p + 1, at], (16, 128))
                    z = x + e
                    q = e * e
                    if mask is not None:
                        z = jnp.where(mask, z, 0.0)
                        q = jnp.where(mask, q, 0.0)
                    zs[t, here, at] = z.astype(BF16)
                    sqs[t, here, :] += q

    def first_layer(ts, k, width):
        at = pl.ds(pl.multiple_of(k * KC, 128), width)
        left = jnp.concatenate([zs[t, :, at] for t in ts], axis=0)
        acc[...] += jnp.dot(left, w1s[at, :], preferred_element_type=F32)

    eye = jnp.where(
        lax.broadcasted_iota(I32, (ROWS, 128), 0) == lax.broadcasted_iota(I32, (ROWS, 128), 1), 1.0, 0.0
    )
    tail_mask = lax.broadcasted_iota(I32, (16, 128), 1) < WIDTH - 3072

    def stats_of(t):
        sq = jnp.sum(sqs[t], axis=1, keepdims=True)
        row_sq = jnp.sum(eye * sq, axis=0, keepdims=True)
        src = jnp.sum(srcs[t], axis=1, keepdims=True)
        row_src = jnp.sum(jnp.where(lane8 // 16 == row8, src, 0.0), axis=0, keepdims=True)
        return jnp.where(row8 == 0, row_sq, jnp.where(row8 == 1, row_src, 0.0))

    def toward(move):
        (dx, dy) = move
        return (pts, ((my + dy + 4) % 4) * 8 + zh * 4 + (mx + dx + 4) % 4)

    def partial_copy(n):
        return remote(psend.at[n], precv.at[n], p_ss.at[n], p_rs.at[n], toward(TREE[n][1]))

    def stat_copy(n):
        return remote(ssend.at[n], srecv.at[n], s_ss.at[n], s_rs.at[n], toward(TREE[n][1]))

    def gathered(n, i, t):
        value, tile = acc[i * ROWS:(i + 1) * ROWS, :], stats_of(t)
        for child in CHILDREN[n]:
            partial_copy(child).wait_recv()
            stat_copy(child).wait_recv()
            value += precv[child].astype(F32)
            tile += srecv[child]
        return value.astype(BF16), tile

    loads[0].wait()
    loads[1].wait()

    for s in range(4):
        ts = [((my + b + 4) % 4) * 4 + (mx + a + 4) % 4 for (a, b), _ in TREE[4 * s:4 * s + 4]]
        acc[...] = jnp.zeros_like(acc)
        noise(ts, 0, KC, None)

        def inner(k, ts=ts):
            first_layer(ts, k - 1, KC)
            noise(ts, k, KC, None)

        each(1, 12, inner)
        first_layer(ts, 11, KC)
        noise(ts, 12, 128, tail_mask)
        first_layer(ts, 12, 128)
        if s == 0:
            pl.semaphore_wait(barrier, XY - 1 + 5)
        for i, t in enumerate(ts):
            n = 4 * s + i
            value, tile = gathered(n, i, t)
            if n < XY - 1:
                psend[n] = value
                ssend[n] = tile
                partial_copy(n).start()
                stat_copy(n).start()
            else:
                zsend[...] = value
                tsend[...] = tile

    z_copy = remote(zsend, zrecv, z_ss.at[0], z_rs.at[0], zpeer)
    t_copy = remote(tsend, trecv, z_ss.at[1], z_rs.at[1], zpeer)
    z_copy.start()
    t_copy.start()
    loads[2].wait()
    z_copy.wait_recv()
    t_copy.wait_recv()

    pre = (zsend[...].astype(F32) + zrecv[...].astype(F32)) + b1_ref[...]
    h1 = jnp.tanh(pre).astype(BF16)
    h1s[...] = h1
    two = jnp.tanh(
        lax.dot_general(h1, w2s[...], (((1,), (1,)), ((), ())), preferred_element_type=F32)
    ).astype(BF16)
    stat = tsend[...] + trecv[...]
    sq = jnp.sum(eye * stat[0:1, :], axis=1, keepdims=True) * 0.25
    src = jnp.sum(eye * stat[1:2, :], axis=1, keepdims=True) / math.sqrt(D)
    two_float = two.astype(F32)
    w3 = w3_ref[...].astype(F32)
    value = 0.0625 * jnp.sum(two_float * w3, axis=1, keepdims=True)
    stein = (sq - D) / 64.0
    prod = jnp.broadcast_to(stein * value, (ROWS, 128)).reshape(4, 16, 128)
    residual = jnp.broadcast_to(jnp.sum(prod, axis=1, keepdims=True), (4, 16, 128)).reshape(ROWS, 128) - src
    for n in range(2):
        @pl.when(zh == n)
        def _():
            first = lax.broadcasted_iota(I32, (1, 128), 1) == 0
            res_ref[0:1, :] = jnp.where(first, residual[32 * n:32 * n + 1, :], residual[32 * n + 16:32 * n + 17, :])

    dval = residual * stein
    dpre2 = (0.0625 * dval[:, 0:1] * w3 * (1.0 - two_float * two_float)).astype(BF16)
    back = jnp.dot(dpre2, w2s[...], preferred_element_type=F32)
    one_float = h1.astype(F32)
    dpre1 = (back * (1.0 - one_float * one_float)).astype(BF16)
    for j in range(4):
        part = dpre1[:, 256 * j:256 * j + 256]
        dbuf[j] = part
        dall[j, me] = part
        h2s[j] = two[:, 256 * j:256 * j + 256]
        d2s[j] = dpre2[:, 256 * j:256 * j + 256]

    def gather_copy(j, t, slot):
        return remote(dbuf.at[j], dall.at[j, slot], a_ss.at[j * XY + t], a_rs.at[j * XY + slot], plane(t))

    inside, upper = zlo * (3 - zlo) // 2, zlo // 2

    def order(q):
        base = (1 - inside) * (3 - q) + inside * ((q % 2) * (q // 2) + (1 - q % 2) * (3 - q // 2))
        return upper * 3 + (1 - 2 * upper) * base

    for q in range(4):
        each(1, XY, lambda p, q=q: gather_copy(order(q), (me + p) % XY, me).start())

    lane64 = lax.broadcasted_iota(I32, (ROWS, 128), 1)
    high = dval.astype(BF16)
    low = (dval - high.astype(F32)).astype(BF16)
    zero = jnp.zeros_like(dval)
    pick0 = jnp.where(lane64 == 0, 1.0, zero).astype(BF16)
    pick1 = jnp.where(lane64 == 1, high.astype(F32), jnp.where(lane64 == 2, low.astype(F32), zero)).astype(BF16)
    rows_of = (((0,), (0,)), ((), ()))
    half = pl.ds(pl.multiple_of(zh * 128, 128), 128)
    for j in range(4):
        main = lax.dot_general(d2s[j, :, half], h1, rows_of, preferred_element_type=F32)
        more = lax.dot_general(dbuf[j, :, half], pick0, rows_of, preferred_element_type=F32)
        more += lax.dot_general(h2s[j, :, half], pick1, rows_of, preferred_element_type=F32)
        gbuf[j, :, 0:HID] = main.astype(BF16)
        gbuf[j, :, HID:WIDE] = more.astype(BF16)
    grecv[me] = gbuf[my, pl.ds(pl.multiple_of(mx * 32, 32), 32), :]

    def small_copy(t, slot):
        mine = gbuf.at[t // 4, pl.ds(pl.multiple_of((t % 4) * 32, 32), 32)]
        return remote(mine, grecv.at[slot], g_ss.at[t], g_rs.at[slot], plane(t))

    each(1, XY, lambda p: small_copy((me + p) % XY, me).start())

    def core_copy(n):
        return remote(bsend.at[n], brecv.at[n], b_ss.at[n], b_rs.at[n], sibling)

    def chunk(j):
        def there(p):
            slot = (me + p) % XY
            gather_copy(j, slot, slot).wait_recv()

        each(1, XY, there)
        for n, c in enumerate((1 - core, core)):
            block = dall[j, :, :, pl.ds(pl.multiple_of(c * 128, 128), 128)].reshape(XY * ROWS, 128)
            dt[128 * n:128 * n + 128, :] = jnp.transpose(block)

        def sub(b):
            at = pl.ds(pl.multiple_of(b * SUB, 128), SUB)
            right = zs[:, :, at].reshape(XY * ROWS, SUB)
            part = jnp.dot(dt[...], right, preferred_element_type=F32)
            n = j * NSUB + b
            bsend[n] = part[0:128].astype(BF16)
            core_copy(n).start()
            own[n] = part[128:256]

        each(0, NSUB, sub)

    def right_copy(n):
        return remote(lsend.at[n], lrecv.at[n], l_ss.at[n], l_rs.at[n], chip(zlo + 1))

    def left_copy(n):
        return remote(rsend.at[n], rrecv.at[n], r_ss.at[n], r_rs.at[n], chip(zlo - 1))

    def chip_sum(n):
        core_copy(n).wait_recv()
        return own[n] + brecv[n].astype(F32)

    def go_right(t, b):
        n = t * NSUB + b
        tmp[...] = chip_sum((3 - t) * NSUB + b)

        @pl.when(zlo > 0)
        def _():
            remote(lsend.at[n], lrecv.at[n], l_ss.at[n], l_rs.at[n], chip(zlo - 1)).wait_recv()
            tmp[...] += lrecv[n].astype(F32)

        lsend[n] = tmp[...].astype(BF16)
        right_copy(n).start()

    def go_left(t, b):
        n = t * NSUB + b
        tmp[...] = chip_sum(n)

        @pl.when(zlo < 3)
        def _():
            remote(rsend.at[n], rrecv.at[n], r_ss.at[n], r_rs.at[n], chip(zlo + 1)).wait_recv()
            tmp[...] += rrecv[n].astype(F32)

        rsend[n] = tmp[...].astype(BF16)
        left_copy(n).start()

    def onward(n):
        r, l = n - LAG * upper, n - LAG * (1 - upper)

        @pl.when((r >= 0) & (r < (3 - zlo) * NSUB))
        def _():
            go_right(r // NSUB, r % NSUB)

        @pl.when((l >= 0) & (l < zlo * NSUB))
        def _():
            go_left(l // NSUB, l % NSUB)

    def columns(q):
        chunk(order(q))
        lo = (1 - inside) * q * NSUB
        hi = (1 - inside) * (q * NSUB + NSUB) + inside * (q // 2) * (1 - q % 2) * (2 * NSUB + LAG)

        @pl.when(q < 3)
        def _():
            each(lo, hi, onward)

    each(0, 4, columns)

    def small_there(p):
        slot = (me + p) % XY
        small_copy(slot, slot).wait_recv()

    each(1, XY, small_there)
    for r in range(2):
        at = slice(16 * r, 16 * r + 16)
        tot = grecv[0, at, :].astype(F32)
        for n in range(1, XY):
            tot += grecv[n, at, :].astype(F32)
        gtot[at, :] = tot
    theirs = pl.ds(pl.multiple_of(16 * (1 - core), 16), 16)
    mine = pl.ds(pl.multiple_of(16 * core, 16), 16)
    hsend[...] = gtot[theirs, :].astype(BF16)
    h_copy = remote(hsend, hrecv, h_ss.at[0], h_rs.at[0], sibling)
    h_copy.start()

    def across(z, slot):
        return remote(csend, crecv.at[slot], c_ss.at[z], c_rs.at[slot], chip(z))

    h_copy.wait_recv()
    total = (gtot[mine, :] + hrecv[...].astype(F32)).astype(BF16)
    csend[...] = total
    crecv[zlo] = total
    for p in (1, 2, 3):
        across((zlo + p) % 4, zlo).start()
    for p in (1, 2, 3):
        across((zlo + p) % 4, (zlo + p) % 4).wait_recv()
    total = crecv[0].astype(F32)
    for n in range(1, 4):
        total += crecv[n].astype(F32)
    fsend[...] = total
    gtot[mine, :] = total
    f_copy = remote(fsend, frecv, h_ss.at[1], h_rs.at[1], sibling)
    f_copy.start()
    f_copy.wait_recv()
    gtot[theirs, :] = frecv[...]
    g2_ref[...] = gtot[:, 0:HID]
    small = gtot[:, HID:WIDE]
    eye32 = eye[0:32, :]
    res_ref[2:3, :] = jnp.sum(eye32 * small[:, 0:1], axis=0, keepdims=True)
    res_ref[3:4, :] = 0.0625 * jnp.sum(eye32 * (small[:, 1:2] + small[:, 2:3]), axis=0, keepdims=True)

    def finish(b):
        tmp[...] = chip_sum(zlo * NSUB + b)

        @pl.when(zlo > 0)
        def _():
            n = (3 - zlo) * NSUB + b
            remote(lsend.at[n], lrecv.at[n], l_ss.at[n], l_rs.at[n], chip(zlo - 1)).wait_recv()
            tmp[...] += lrecv[n].astype(F32)

        @pl.when(zlo < 3)
        def _():
            n = zlo * NSUB + b
            remote(rsend.at[n], rrecv.at[n], r_ss.at[n], r_rs.at[n], chip(zlo + 1)).wait_recv()
            tmp[...] += rrecv[n].astype(F32)

        grad_ref[:, pl.ds(pl.multiple_of(b * SUB, 128), SUB)] = tmp[...].astype(BF16)

    each(0, NSUB, finish)

    def left_plane(p):
        t = (me + p) % XY
        small_copy(t, me).wait_send()
        for j in range(4):
            gather_copy(j, t, me).wait_send()

    each(1, XY, left_plane)
    for n in range(XY - 1):
        partial_copy(n).wait_send()
        stat_copy(n).wait_send()
    z_copy.wait_send()
    t_copy.wait_send()
    h_copy.wait_send()
    f_copy.wait_send()
    for p in (1, 2, 3):
        across((zlo + p) % 4, zlo).wait_send()
    each(0, 4 * NSUB, lambda n: core_copy(n).wait_send())
    each(0, (3 - zlo) * NSUB, lambda n: right_copy(n).wait_send())
    each(0, zlo * NSUB, lambda n: left_copy(n).wait_send())


def shards(point_seed, pert_seed, source_coef, w1, b1, w2, w3):
    coef = jnp.pad(source_coef.reshape(1, WIDTH), ((0, 0), (0, LANES - WIDTH)))
    w1t = w1.T
    tail = jnp.pad(w1t[3072:], ((0, LANES - WIDTH), (0, 0)))
    vmem = pl.BlockSpec(memory_space=pltpu.VMEM)
    anyw = pl.BlockSpec(memory_space=pl.ANY)
    dma = lambda n: pltpu.SemaphoreType.DMA((n,))
    v = pltpu.VMEM
    n15, n20 = 3 * NSUB, 4 * NSUB
    residual, grad, small = pl.pallas_call(
        kernel,
        name="pinn_step",
        out_shape=(
            jax.ShapeDtypeStruct((8, 128), F32),
            jax.ShapeDtypeStruct((128, LANES), BF16),
            jax.ShapeDtypeStruct((32, HID), F32),
        ),
        in_specs=[vmem, vmem, vmem, anyw, anyw, vmem, anyw, vmem],
        out_specs=(vmem, vmem, vmem),
        scratch_shapes=[
            v((XY, ROWS, 128), I32), v((64, 128), I32), v((LANES, HID), BF16), v((HID, HID), BF16), v((XY, ROWS, LANES), BF16),
            v((XY, 8, LANES), F32), v((2, 8, LANES), I32), v((XY, ROWS, 128), F32), v((XY, 8, 128), F32),
            v((256, HID), F32),
            v((XY, ROWS, HID), BF16), v((XY, ROWS, HID), BF16), v((XY, 8, 128), F32), v((XY, 8, 128), F32),
            v((ROWS, HID), BF16), v((ROWS, HID), BF16), v((8, 128), F32), v((8, 128), F32),
            v((ROWS, HID), BF16), v((4, ROWS, 256), BF16), v((4, ROWS, 256), BF16), v((4, ROWS, 256), BF16),
            v((4, XY, ROWS, 256), BF16), v((256, XY * ROWS), BF16),
            v((n20, 128, SUB), F32), v((n20, 128, SUB), BF16), v((n20, 128, SUB), BF16), v((128, SUB), F32),
            v((n15, 128, SUB), BF16), v((n15, 128, SUB), BF16), v((n15, 128, SUB), BF16), v((n15, 128, SUB), BF16),
            v((4, 128, WIDE), BF16), v((XY, 32, WIDE), BF16), v((32, WIDE), F32),
            v((16, WIDE), BF16), v((16, WIDE), BF16), v((16, WIDE), BF16), v((4, 16, WIDE), BF16),
            v((16, WIDE), F32), v((16, WIDE), F32),
            dma(3), dma(XY), dma(XY), dma(XY), dma(XY), dma(2), dma(2), dma(4 * XY), dma(4 * XY), dma(n20), dma(n20),
            dma(n15), dma(n15), dma(n15), dma(n15), dma(XY), dma(XY), dma(2), dma(2), dma(4), dma(4),
        ],
        compiler_params=pltpu.CompilerParams(
            collective_id=0, has_side_effects=True, vmem_limit_bytes=66_000_000
        ),
    )(pert_seed.T, point_seed.reshape(1, 64), coef, w1t, tail, b1.reshape(1, HID), w2, w3.reshape(1, HID))
    return residual[0, 0:2], grad[:, :WIDTH], small, residual[2, 0:32], residual[3, 0:32]


def solution(mesh):
    return jax.shard_map(
        shards,
        mesh=mesh,
        in_specs=(P("pts"), P("pts", None), P("coord"), P(None, "coord"), P(), P(), P()),
        out_specs=(
            P(("pts", "coord")),
            P("pts", "coord"),
            P("coord", None),
            P("coord"),
            P("coord"),
        ),
        check_vma=False,
    )
```

```python
import math

import jax
import jax.numpy as jnp
from jax import lax
from jax.experimental import pallas as pl
from jax.experimental.pallas import tpu as pltpu
from jax.sharding import PartitionSpec as P

D = 100000
HASH = 73244475
MESH = pl.DeviceIdType.MESH
F32, BF16, I32 = jnp.float32, jnp.bfloat16, jnp.int32
SINE = (1.5707962900223675, -0.6459633598658464, 0.07968848054018324, -0.004672227923047835, 0.00015082056445751214)
LOW = 8388607
UNIT = 1.0 / 8388608.0

XY = 16
ROWS = 64
HID = 1024
WIDTH = 3125
LANES = 3200
SUB = 640
NSUB = LANES // SUB
LAG = 2
KC = 256
WIDE = HID + 128

TREE = (
    ((2, 2), (1, 0)), ((2, 1), (0, 1)), ((2, -1), (-1, 0)), ((-1, 2), (0, -1)),
    ((1, 2), (0, 1)), ((2, 0), (1, 0)), ((0, 2), (0, -1)), ((-1, -1), (-1, 0)),
    ((1, 1), (1, 0)), ((-1, 1), (0, 1)), ((1, -1), (0, -1)), ((0, -1), (0, -1)),
    ((1, 0), (1, 0)), ((-1, 0), (-1, 0)), ((0, 1), (0, 1)), ((0, 0), None),
)


def lands(n):
    (a, b), move = TREE[n]
    if move is None:
        return None
    return tuple((v + 1) % 4 - 1 for v in (a - move[0], b - move[1]))


CHILDREN = [[m for m in range(XY) if lands(m) == TREE[n][0]] for n in range(XY)]
assert all(m // 4 < n // 4 for n in range(XY - 1) for m in CHILDREN[n])


def shuffle_bits(v):
    return v ^ lax.shift_right_logical(v, jnp.full_like(v, 16))


def rounds(v):
    v = shuffle_bits(v * HASH)
    return shuffle_bits(v * HASH)


def sine(y, scale):
    t = y * y
    acc = t * (SINE[4] * scale) + (SINE[3] * scale)
    for c in (SINE[2], SINE[1], SINE[0]):
        acc = acc * t + (c * scale)
    return acc * y


def kernel(
    pert_ref, point_ref, coef_ref, w1_ref, w1t_ref, b1_ref, w2_ref, w3_ref,
    res_ref, grad_ref, g2_ref,
    seed_ref, pseed_ref, w1s, w2s, zs, xs, hs, sqs, srcs, acc,
    psend, precv, ssend, srecv, zsend, zrecv, tsend, trecv,
    h1s, h2s, d2s, dbuf, dall, dt, own, bsend, brecv, tmp, lsend, lrecv, rsend, rrecv,
    gbuf, grecv, gtot, hsend, hrecv, csend, crecv, fsend, frecv,
    load_sem, p_ss, p_rs, s_ss, s_rs, z_ss, z_rs, a_ss, a_rs, b_ss, b_rs,
    l_ss, l_rs, r_ss, r_rs, g_ss, g_rs, h_ss, h_rs, c_ss, c_rs,
):
    pts, coord = lax.axis_index("pts"), lax.axis_index("coord")
    zlo, core = pts // 2, pts % 2
    mx, zh, my = coord % 4, (coord // 4) % 2, coord // 8
    me = my * 4 + mx

    def plane(t):
        return (pts, (t // 4) * 8 + zh * 4 + t % 4)

    zpeer = (pts, coord + 4 - 8 * zh)
    sibling = (pts + 1 - 2 * core, coord)

    def chip(z):
        return (z * 2 + core, coord)

    def remote(src, dst, ss, rs, device):
        return pltpu.make_async_remote_copy(src, dst, ss, rs, device_id=device, device_id_type=MESH)

    def each(lo, hi, body):
        def run(i, c):
            body(i)
            return c

        lax.fori_loop(lo, hi, run, 0)

    loads = [
        pltpu.make_async_copy(w1_ref.at[pl.ds(0, 3072)], w1s.at[pl.ds(0, 3072)], load_sem.at[0]),
        pltpu.make_async_copy(w1t_ref, w1s.at[pl.ds(3072, 128)], load_sem.at[1]),
        pltpu.make_async_copy(w2_ref, w2s, load_sem.at[2]),
    ]
    for c in loads:
        c.start()
    barrier = pltpu.get_barrier_semaphore()

    def greet(device):
        pl.semaphore_signal(barrier, inc=1, device_id=device, device_id_type=MESH)

    each(1, XY, lambda p: greet(plane((me + p) % XY)))
    greet(zpeer)
    greet(sibling)
    for p in (1, 2, 3):
        greet(chip((zlo + p) % 4))

    for n in range(64):
        pos = ((n // 16) * 4 + (n // 2) % 4, ((n // 8) % 2) * 2 + n % 2)
        seed = jnp.broadcast_to(pert_ref[:, n:n + 1], (16, 128))
        seed_ref[pos[0], 16 * pos[1]:16 * pos[1] + 16, :] = shuffle_bits(seed)
    r64 = lax.broadcasted_iota(I32, (64, 64), 0)
    place = (((r64 // 16) * 2 + (r64 // 2) % 2) * 4 + (r64 // 4) % 4) * 2 + r64 % 2
    spread = jnp.where(place == lax.broadcasted_iota(I32, (64, 64), 1), point_ref[...].astype(F32), 0.0)
    spread = jnp.sum(spread, axis=1, keepdims=True).astype(I32)
    pseed_ref[...] = shuffle_bits(jnp.broadcast_to(spread, (64, 128)))

    srcs[...] = jnp.zeros_like(srcs)
    lane8 = lax.broadcasted_iota(I32, (8, 128), 1)
    row8 = lax.broadcasted_iota(I32, (8, 128), 0)

    def points(k):
        at = pl.ds(pl.multiple_of(k * 128, 128), 128)
        col = (coord * WIDTH + k * 128 + lane8) * 4
        for n in range(3):
            h = rounds(shuffle_bits(col + n))
            if n < 2:
                hs[n, :, at] = shuffle_bits(h)
        h = shuffle_bits(h)
        coef = jnp.broadcast_to(coef_ref[:, at], (8, 128))
        for g in range(8):
            v = rounds(h ^ pseed_ref[8 * g:8 * g + 8, :])
            t = (v & LOW).astype(F32) + (0.5 - 4194304.0)
            x = t * (2.0 * UNIT)
            y = t * (4.0 * UNIT)
            fold = 1.0 - jnp.abs(jnp.abs(y) - 1.0)
            s = coef * sine(jnp.where(y < 0, -fold, fold), 1.0)
            for i in range(2):
                xs[g * 2 + i, 0:4, at] = x[4 * i:4 * i + 4]
                srcs[g * 2 + i, 0:4, :] += s[4 * i:4 * i + 4]

    each(0, LANES // 128, points)

    def target(s, n):
        power = 1 + 3 * n + 9 * (n * (n - 1) // 2) + 27 * (n * (n - 1) * (n - 2) // 6)
        a, b = (sum((TREE[4 * s + i][0][d] % 4) * 4**i for i in range(4)) for d in range(2))
        return ((my + (b // power) % 4) % 4) * 4 + (mx + (a // power) % 4) % 4

    def noise(t):
        for p in range(4):
            here = pl.ds(p * 16, 16)
            seed = seed_ref[t, here, :]
            squares = None
            for l in range(LANES // 128):
                at = pl.ds(l * 128, 128)
                h0, h1 = hs[0, :, at], hs[1, :, at]
                h0 = jnp.concatenate([h0, h0], axis=0)
                h1 = jnp.concatenate([h1, h1], axis=0)
                u0 = ((rounds(h0 ^ seed) & LOW).astype(F32) + 0.5) * UNIT
                w = jnp.maximum(-2.0 * jnp.log(u0), 1e-9)
                r = w * lax.rsqrt(w)
                a = (rounds(h1 ^ seed) & LOW).astype(F32) + (0.5 - 4194304.0)
                y = (jnp.abs(a) - 2097152.0) * (4.0 * UNIT)
                e = r * sine(y, 2.0)
                z = jnp.broadcast_to(xs[t, p:p + 1, at], (16, 128)) + e
                q = e * e
                if l == LANES // 128 - 1:
                    z = jnp.where(tail_mask, z, 0.0)
                    q = jnp.where(tail_mask, q, 0.0)
                zs[t, here, at] = z.astype(BF16)
                squares = q if squares is None else squares + q
            sqs[t, here, :] = squares

    def first_layer(s, n):
        at = pl.ds(pl.multiple_of(n * 256, 256), 256)
        left = jnp.concatenate([zs[target(s, i)] for i in range(4)], axis=0)
        acc[:, at] = jnp.dot(left, w1s[:, at], preferred_element_type=F32)

    eye = jnp.where(
        lax.broadcasted_iota(I32, (ROWS, 128), 0) == lax.broadcasted_iota(I32, (ROWS, 128), 1), 1.0, 0.0
    )
    tail_mask = lax.broadcasted_iota(I32, (16, 128), 1) < WIDTH - 3072

    def stats_of(t):
        sq = jnp.sum(sqs[t], axis=1, keepdims=True)
        row_sq = jnp.sum(eye * sq, axis=0, keepdims=True)
        src = jnp.sum(srcs[t], axis=1, keepdims=True)
        row_src = jnp.sum(jnp.where(lane8 // 16 == row8, src, 0.0), axis=0, keepdims=True)
        return jnp.where(row8 == 0, row_sq, jnp.where(row8 == 1, row_src, 0.0))

    def toward(move):
        (dx, dy) = move
        return (pts, ((my + dy + 4) % 4) * 8 + zh * 4 + (mx + dx + 4) % 4)

    def partial_copy(n):
        return remote(psend.at[n], precv.at[n], p_ss.at[n], p_rs.at[n], toward(TREE[n][1]))

    def stat_copy(n):
        return remote(ssend.at[n], srecv.at[n], s_ss.at[n], s_rs.at[n], toward(TREE[n][1]))

    def gathered(n, i, t):
        value, tile = acc[i * ROWS:(i + 1) * ROWS, :], stats_of(t)
        for child in CHILDREN[n]:
            partial_copy(child).wait_recv()
            stat_copy(child).wait_recv()
            value += precv[child].astype(F32)
            tile += srecv[child]
        return value.astype(BF16), tile

    for s in range(5):
        if s == 1:
            loads[0].wait()
            loads[1].wait()

        def both(n, s=s):
            if s < 4:
                noise(target(s, n))
            if s > 0:
                first_layer(s - 1, n)

        each(0, 4, both)
        if s == 0:
            continue
        if s == 1:
            pl.semaphore_wait(barrier, XY - 1 + 5)
        ts = [target(s - 1, i) for i in range(4)]
        for i, t in enumerate(ts):
            n = 4 * s - 4 + i
            value, tile = gathered(n, i, t)
            if n < XY - 1:
                psend[n] = value
                ssend[n] = tile
                partial_copy(n).start()
                stat_copy(n).start()
            else:
                zsend[...] = value
                tsend[...] = tile

    z_copy = remote(zsend, zrecv, z_ss.at[0], z_rs.at[0], zpeer)
    t_copy = remote(tsend, trecv, z_ss.at[1], z_rs.at[1], zpeer)
    z_copy.start()
    t_copy.start()
    loads[2].wait()
    z_copy.wait_recv()
    t_copy.wait_recv()

    pre = (zsend[...].astype(F32) + zrecv[...].astype(F32)) + b1_ref[...]
    h1 = jnp.tanh(pre).astype(BF16)
    h1s[...] = h1
    two = jnp.tanh(
        lax.dot_general(h1, w2s[...], (((1,), (1,)), ((), ())), preferred_element_type=F32)
    ).astype(BF16)
    stat = tsend[...] + trecv[...]
    sq = jnp.sum(eye * stat[0:1, :], axis=1, keepdims=True) * 0.25
    src = jnp.sum(eye * stat[1:2, :], axis=1, keepdims=True) / math.sqrt(D)
    two_float = two.astype(F32)
    w3 = w3_ref[...].astype(F32)
    value = 0.0625 * jnp.sum(two_float * w3, axis=1, keepdims=True)
    stein = (sq - D) / 64.0
    prod = jnp.broadcast_to(stein * value, (ROWS, 128)).reshape(4, 16, 128)
    residual = jnp.broadcast_to(jnp.sum(prod, axis=1, keepdims=True), (4, 16, 128)).reshape(ROWS, 128) - src
    for n in range(2):
        @pl.when(zh == n)
        def _():
            first = lax.broadcasted_iota(I32, (1, 128), 1) == 0
            res_ref[0:1, :] = jnp.where(first, residual[32 * n:32 * n + 1, :], residual[32 * n + 16:32 * n + 17, :])

    dval = residual * stein
    dpre2 = (0.0625 * dval[:, 0:1] * w3 * (1.0 - two_float * two_float)).astype(BF16)
    back = jnp.dot(dpre2, w2s[...], preferred_element_type=F32)
    one_float = h1.astype(F32)
    dpre1 = (back * (1.0 - one_float * one_float)).astype(BF16)
    for j in range(4):
        part = dpre1[:, 256 * j:256 * j + 256]
        dbuf[j] = part
        dall[j, me] = part
        h2s[j] = two[:, 256 * j:256 * j + 256]
        d2s[j] = dpre2[:, 256 * j:256 * j + 256]

    def gather_copy(j, t, slot):
        return remote(dbuf.at[j], dall.at[j, slot], a_ss.at[j * XY + t], a_rs.at[j * XY + slot], plane(t))

    inside, upper = zlo * (3 - zlo) // 2, zlo // 2

    def order(q):
        base = (1 - inside) * (3 - q) + inside * ((q % 2) * (q // 2) + (1 - q % 2) * (3 - q // 2))
        return upper * 3 + (1 - 2 * upper) * base

    for q in range(4):
        each(1, XY, lambda p, q=q: gather_copy(order(q), (me + p) % XY, me).start())

    lane64 = lax.broadcasted_iota(I32, (ROWS, 128), 1)
    high = dval.astype(BF16)
    low = (dval - high.astype(F32)).astype(BF16)
    zero = jnp.zeros_like(dval)
    pick0 = jnp.where(lane64 == 0, 1.0, zero).astype(BF16)
    pick1 = jnp.where(lane64 == 1, high.astype(F32), jnp.where(lane64 == 2, low.astype(F32), zero)).astype(BF16)
    rows_of = (((0,), (0,)), ((), ()))
    half = pl.ds(pl.multiple_of(zh * 128, 128), 128)
    for j in range(4):
        main = lax.dot_general(d2s[j, :, half], h1, rows_of, preferred_element_type=F32)
        more = lax.dot_general(dbuf[j, :, half], pick0, rows_of, preferred_element_type=F32)
        more += lax.dot_general(h2s[j, :, half], pick1, rows_of, preferred_element_type=F32)
        gbuf[j, :, 0:HID] = main.astype(BF16)
        gbuf[j, :, HID:WIDE] = more.astype(BF16)
    grecv[me] = gbuf[my, pl.ds(pl.multiple_of(mx * 32, 32), 32), :]

    def small_copy(t, slot):
        mine = gbuf.at[t // 4, pl.ds(pl.multiple_of((t % 4) * 32, 32), 32)]
        return remote(mine, grecv.at[slot], g_ss.at[t], g_rs.at[slot], plane(t))

    each(1, XY, lambda p: small_copy((me + p) % XY, me).start())

    def core_copy(n):
        return remote(bsend.at[n], brecv.at[n], b_ss.at[n], b_rs.at[n], sibling)

    def right_copy(n):
        return remote(lsend.at[n], lrecv.at[n], l_ss.at[n], l_rs.at[n], chip(zlo + 1))

    def left_copy(n):
        return remote(rsend.at[n], rrecv.at[n], r_ss.at[n], r_rs.at[n], chip(zlo - 1))

    def chip_sum(n):
        core_copy(n).wait_recv()
        return own[n] + brecv[n].astype(F32)

    def go_right(t, b):
        n = t * NSUB + b
        tmp[...] = chip_sum((3 - t) * NSUB + b)

        @pl.when(zlo > 0)
        def _():
            remote(lsend.at[n], lrecv.at[n], l_ss.at[n], l_rs.at[n], chip(zlo - 1)).wait_recv()
            tmp[...] += lrecv[n].astype(F32)

        lsend[n] = tmp[...].astype(BF16)
        right_copy(n).start()

    def go_left(t, b):
        n = t * NSUB + b
        tmp[...] = chip_sum(n)

        @pl.when(zlo < 3)
        def _():
            remote(rsend.at[n], rrecv.at[n], r_ss.at[n], r_rs.at[n], chip(zlo + 1)).wait_recv()
            tmp[...] += rrecv[n].astype(F32)

        rsend[n] = tmp[...].astype(BF16)
        left_copy(n).start()

    def onward(n):
        r, l = n - LAG * upper, n - LAG * (1 - upper)

        @pl.when((r >= 0) & (r < (3 - zlo) * NSUB))
        def _():
            go_right(r // NSUB, r % NSUB)

        @pl.when((l >= 0) & (l < zlo * NSUB))
        def _():
            go_left(l // NSUB, l % NSUB)

    def chunk(j, after):
        def there(p):
            slot = (me + p) % XY
            gather_copy(j, slot, slot).wait_recv()

        each(1, XY, there)
        for n, c in enumerate((1 - core, core)):
            block = dall[j, :, :, pl.ds(pl.multiple_of(c * 128, 128), 128)].reshape(XY * ROWS, 128)
            dt[128 * n:128 * n + 128, :] = jnp.transpose(block)

        def sub(b):
            at = pl.ds(pl.multiple_of(b * SUB, 128), SUB)
            right = zs[:, :, at].reshape(XY * ROWS, SUB)
            part = jnp.dot(dt[...], right, preferred_element_type=F32)
            n = j * NSUB + b
            bsend[n] = part[0:128].astype(BF16)
            core_copy(n).start()
            own[n] = part[128:256]
            after(b)

        each(0, NSUB, sub)

    def columns(q):
        def after(b):
            @pl.when((inside == 0) & (q < 3) & (b >= 2))
            def _():
                onward(q * NSUB + b - 2)

        chunk(order(q), after)
        lo = (1 - inside) * (q * NSUB + NSUB - 2)
        hi = (1 - inside) * (q * NSUB + NSUB) + inside * (q // 2) * (1 - q % 2) * (2 * NSUB + LAG)

        @pl.when(q < 3)
        def _():
            each(lo, hi, onward)

    each(0, 4, columns)

    def small_there(p):
        slot = (me + p) % XY
        small_copy(slot, slot).wait_recv()

    each(1, XY, small_there)
    for r in range(2):
        at = slice(16 * r, 16 * r + 16)
        tot = grecv[0, at, :].astype(F32)
        for n in range(1, XY):
            tot += grecv[n, at, :].astype(F32)
        gtot[at, :] = tot
    theirs = pl.ds(pl.multiple_of(16 * (1 - core), 16), 16)
    mine = pl.ds(pl.multiple_of(16 * core, 16), 16)
    hsend[...] = gtot[theirs, :].astype(BF16)
    h_copy = remote(hsend, hrecv, h_ss.at[0], h_rs.at[0], sibling)
    h_copy.start()

    def across(z, slot):
        return remote(csend, crecv.at[slot], c_ss.at[z], c_rs.at[slot], chip(z))

    h_copy.wait_recv()
    total = (gtot[mine, :] + hrecv[...].astype(F32)).astype(BF16)
    csend[...] = total
    crecv[zlo] = total
    for p in (1, 2, 3):
        across((zlo + p) % 4, zlo).start()
    for p in (1, 2, 3):
        across((zlo + p) % 4, (zlo + p) % 4).wait_recv()
    total = crecv[0].astype(F32)
    for n in range(1, 4):
        total += crecv[n].astype(F32)
    fsend[...] = total
    gtot[mine, :] = total
    f_copy = remote(fsend, frecv, h_ss.at[1], h_rs.at[1], sibling)
    f_copy.start()
    f_copy.wait_recv()
    gtot[theirs, :] = frecv[...]
    g2_ref[...] = gtot[:, 0:HID]
    small = gtot[:, HID:WIDE]
    eye32 = eye[0:32, :]
    res_ref[2:3, :] = jnp.sum(eye32 * small[:, 0:1], axis=0, keepdims=True)
    res_ref[3:4, :] = 0.0625 * jnp.sum(eye32 * (small[:, 1:2] + small[:, 2:3]), axis=0, keepdims=True)

    def finish(b):
        tmp[...] = chip_sum(zlo * NSUB + b)

        @pl.when(zlo > 0)
        def _():
            n = (3 - zlo) * NSUB + b
            remote(lsend.at[n], lrecv.at[n], l_ss.at[n], l_rs.at[n], chip(zlo - 1)).wait_recv()
            tmp[...] += lrecv[n].astype(F32)

        @pl.when(zlo < 3)
        def _():
            n = zlo * NSUB + b
            remote(rsend.at[n], rrecv.at[n], r_ss.at[n], r_rs.at[n], chip(zlo + 1)).wait_recv()
            tmp[...] += rrecv[n].astype(F32)

        grad_ref[:, pl.ds(pl.multiple_of(b * SUB, 128), SUB)] = tmp[...].astype(BF16)

    each(0, NSUB, finish)

    def left_plane(p):
        t = (me + p) % XY
        small_copy(t, me).wait_send()
        for j in range(4):
            gather_copy(j, t, me).wait_send()

    each(1, XY, left_plane)
    for n in range(XY - 1):
        partial_copy(n).wait_send()
        stat_copy(n).wait_send()
    z_copy.wait_send()
    t_copy.wait_send()
    h_copy.wait_send()
    f_copy.wait_send()
    for p in (1, 2, 3):
        across((zlo + p) % 4, zlo).wait_send()
    each(0, 4 * NSUB, lambda n: core_copy(n).wait_send())
    each(0, (3 - zlo) * NSUB, lambda n: right_copy(n).wait_send())
    each(0, zlo * NSUB, lambda n: left_copy(n).wait_send())


def shards(point_seed, pert_seed, source_coef, w1, b1, w2, w3):
    coef = jnp.pad(source_coef.reshape(1, WIDTH), ((0, 0), (0, LANES - WIDTH)))
    w1t = w1.T
    tail = jnp.pad(w1t[3072:], ((0, LANES - WIDTH), (0, 0)))
    vmem = pl.BlockSpec(memory_space=pltpu.VMEM)
    anyw = pl.BlockSpec(memory_space=pl.ANY)
    dma = lambda n: pltpu.SemaphoreType.DMA((n,))
    v = pltpu.VMEM
    n15, n20 = 3 * NSUB, 4 * NSUB
    residual, grad, small = pl.pallas_call(
        kernel,
        name="pinn_step",
        out_shape=(
            jax.ShapeDtypeStruct((8, 128), F32),
            jax.ShapeDtypeStruct((128, LANES), BF16),
            jax.ShapeDtypeStruct((32, HID), F32),
        ),
        in_specs=[vmem, vmem, vmem, anyw, anyw, vmem, anyw, vmem],
        out_specs=(vmem, vmem, vmem),
        scratch_shapes=[
            v((XY, ROWS, 128), I32), v((64, 128), I32), v((LANES, HID), BF16), v((HID, HID), BF16), v((XY, ROWS, LANES), BF16),
            v((XY, 8, LANES), F32), v((2, 8, LANES), I32), v((XY, ROWS, 128), F32), v((XY, 8, 128), F32),
            v((256, HID), F32),
            v((XY, ROWS, HID), BF16), v((XY, ROWS, HID), BF16), v((XY, 8, 128), F32), v((XY, 8, 128), F32),
            v((ROWS, HID), BF16), v((ROWS, HID), BF16), v((8, 128), F32), v((8, 128), F32),
            v((ROWS, HID), BF16), v((4, ROWS, 256), BF16), v((4, ROWS, 256), BF16), v((4, ROWS, 256), BF16),
            v((4, XY, ROWS, 256), BF16), v((256, XY * ROWS), BF16),
            v((n20, 128, SUB), F32), v((n20, 128, SUB), BF16), v((n20, 128, SUB), BF16), v((128, SUB), F32),
            v((n15, 128, SUB), BF16), v((n15, 128, SUB), BF16), v((n15, 128, SUB), BF16), v((n15, 128, SUB), BF16),
            v((4, 128, WIDE), BF16), v((XY, 32, WIDE), BF16), v((32, WIDE), F32),
            v((16, WIDE), BF16), v((16, WIDE), BF16), v((16, WIDE), BF16), v((4, 16, WIDE), BF16),
            v((16, WIDE), F32), v((16, WIDE), F32),
            dma(3), dma(XY), dma(XY), dma(XY), dma(XY), dma(2), dma(2), dma(4 * XY), dma(4 * XY), dma(n20), dma(n20),
            dma(n15), dma(n15), dma(n15), dma(n15), dma(XY), dma(XY), dma(2), dma(2), dma(4), dma(4),
        ],
        compiler_params=pltpu.CompilerParams(
            collective_id=0, has_side_effects=True, vmem_limit_bytes=66_000_000
        ),
    )(pert_seed.T, point_seed.reshape(1, 64), coef, w1t, tail, b1.reshape(1, HID), w2, w3.reshape(1, HID))
    return residual[0, 0:2], grad[:, :WIDTH], small, residual[2, 0:32], residual[3, 0:32]


def solution(mesh):
    return jax.shard_map(
        shards,
        mesh=mesh,
        in_specs=(P("pts"), P("pts", None), P("coord"), P(None, "coord"), P(), P(), P()),
        out_specs=(
            P(("pts", "coord")),
            P("pts", "coord"),
            P("coord", None),
            P("coord"),
            P("coord"),
        ),
        check_vma=False,
    )
```

```python
import math

import jax
import jax.numpy as jnp
from jax import lax
from jax.experimental import pallas as pl
from jax.experimental.pallas import tpu as pltpu
from jax.sharding import PartitionSpec as P

D = 100000
HASH = 73244475
MESH = pl.DeviceIdType.MESH
F32, BF16, I32 = jnp.float32, jnp.bfloat16, jnp.int32
SINE = (1.5707962900223675, -0.6459633598658464, 0.07968848054018324, -0.004672227923047835, 0.00015082056445751214)
LOW = 8388607
UNIT = 1.0 / 8388608.0

XY = 16
ROWS = 64
HID = 1024
WIDTH = 3125
LANES = 3200
SUB = 640
NSUB = LANES // SUB
LAG = 2
KC = 256
WIDE = HID + 128

TREE = (
    ((2, 2), (1, 0)), ((2, 1), (0, 1)), ((2, -1), (-1, 0)), ((-1, 2), (0, -1)),
    ((1, 2), (0, 1)), ((2, 0), (1, 0)), ((0, 2), (0, -1)), ((-1, -1), (-1, 0)),
    ((1, 1), (1, 0)), ((-1, 1), (0, 1)), ((1, -1), (0, -1)), ((0, -1), (0, -1)),
    ((1, 0), (1, 0)), ((-1, 0), (-1, 0)), ((0, 1), (0, 1)), ((0, 0), None),
)


NEAR = ((1, 1), (-1, -1), (1, 0), (0, 1), (-1, 1), (1, -1), (-1, 0), (0, -1))
RELAY = (((1, 1), (1, 1)), ((1, 1), (0, 1)), ((1, 0), (1, 0)), ((0, 1), (0, 1)), ((-1, -1), (-1, 0)), ((-1, -1), (0, -1)), ((-1, 1), (-1, 0)))
PASSED = tuple(dict.fromkeys(o for o, _ in RELAY))
FAR = tuple(((o[0] + m[0] + 1) % 4 - 1, (o[1] + m[1] + 1) % 4 - 1) for o, m in RELAY)
assert len(set(NEAR + FAR)) == XY - 1 and (0, 0) not in NEAR + FAR


def lands(n):
    (a, b), move = TREE[n]
    if move is None:
        return None
    return tuple((v + 1) % 4 - 1 for v in (a - move[0], b - move[1]))


CHILDREN = [[m for m in range(XY) if lands(m) == TREE[n][0]] for n in range(XY)]
assert all(m // 4 < n // 4 for n in range(XY - 1) for m in CHILDREN[n])


def shuffle_bits(v):
    return v ^ lax.shift_right_logical(v, jnp.full_like(v, 16))


def rounds(v):
    v = shuffle_bits(v * HASH)
    return shuffle_bits(v * HASH)


def sine(y, scale):
    t = y * y
    acc = t * (SINE[4] * scale) + (SINE[3] * scale)
    for c in (SINE[2], SINE[1], SINE[0]):
        acc = acc * t + (c * scale)
    return acc * y


def kernel(
    pert_ref, point_ref, coef_ref, w1_ref, w1t_ref, b1_ref, w2_ref, w3_ref,
    res_ref, grad_ref, g2_ref,
    seed_ref, pseed_ref, w1s, w2s, zs, xs, hs, sqs, srcs, acc,
    psend, precv, ssend, srecv, zsend, zrecv, tsend, trecv,
    h1s, h2s, d2s, dbuf, dall, dt, own, bsend, brecv, tmp, lsend, lrecv, rsend, rrecv,
    gbuf, grecv, gtot, hsend, hrecv, csend, crecv, fsend, frecv,
    load_sem, p_ss, p_rs, s_ss, s_rs, z_ss, z_rs, a_ss, a_rs, b_ss, b_rs,
    l_ss, l_rs, r_ss, r_rs, g_ss, g_rs, h_ss, h_rs, c_ss, c_rs,
):
    pts, coord = lax.axis_index("pts"), lax.axis_index("coord")
    zlo, core = pts // 2, pts % 2
    mx, zh, my = coord % 4, (coord // 4) % 2, coord // 8
    me = my * 4 + mx

    def plane(t):
        return (pts, (t // 4) * 8 + zh * 4 + t % 4)

    zpeer = (pts, coord + 4 - 8 * zh)
    sibling = (pts + 1 - 2 * core, coord)

    def chip(z):
        return (z * 2 + core, coord)

    def remote(src, dst, ss, rs, device):
        return pltpu.make_async_remote_copy(src, dst, ss, rs, device_id=device, device_id_type=MESH)

    def each(lo, hi, body):
        def run(i, c):
            body(i)
            return c

        lax.fori_loop(lo, hi, run, 0)

    loads = [
        pltpu.make_async_copy(w1_ref.at[pl.ds(0, 3072)], w1s.at[pl.ds(0, 3072)], load_sem.at[0]),
        pltpu.make_async_copy(w1t_ref, w1s.at[pl.ds(3072, 128)], load_sem.at[1]),
        pltpu.make_async_copy(w2_ref, w2s, load_sem.at[2]),
    ]
    for c in loads:
        c.start()
    barrier = pltpu.get_barrier_semaphore()

    def greet(device):
        pl.semaphore_signal(barrier, inc=1, device_id=device, device_id_type=MESH)

    each(1, XY, lambda p: greet(plane((me + p) % XY)))
    greet(zpeer)
    greet(sibling)
    for p in (1, 2, 3):
        greet(chip((zlo + p) % 4))

    for n in range(64):
        pos = ((n // 16) * 4 + (n // 2) % 4, ((n // 8) % 2) * 2 + n % 2)
        seed = jnp.broadcast_to(pert_ref[:, n:n + 1], (16, 128))
        seed_ref[pos[0], 16 * pos[1]:16 * pos[1] + 16, :] = shuffle_bits(seed)
    r64 = lax.broadcasted_iota(I32, (64, 64), 0)
    place = (((r64 // 16) * 2 + (r64 // 2) % 2) * 4 + (r64 // 4) % 4) * 2 + r64 % 2
    spread = jnp.where(place == lax.broadcasted_iota(I32, (64, 64), 1), point_ref[...].astype(F32), 0.0)
    spread = jnp.sum(spread, axis=1, keepdims=True).astype(I32)
    pseed_ref[...] = shuffle_bits(jnp.broadcast_to(spread, (64, 128)))

    srcs[...] = jnp.zeros_like(srcs)
    lane8 = lax.broadcasted_iota(I32, (8, 128), 1)
    row8 = lax.broadcasted_iota(I32, (8, 128), 0)

    def points(k):
        at = pl.ds(pl.multiple_of(k * 128, 128), 128)
        col = (coord * WIDTH + k * 128 + lane8) * 4
        for n in range(3):
            h = rounds(shuffle_bits(col + n))
            if n < 2:
                hs[n, :, at] = shuffle_bits(h)
        h = shuffle_bits(h)
        coef = jnp.broadcast_to(coef_ref[:, at], (8, 128))
        for g in range(8):
            v = rounds(h ^ pseed_ref[8 * g:8 * g + 8, :])
            t = (v & LOW).astype(F32) + (0.5 - 4194304.0)
            x = t * (2.0 * UNIT)
            y = t * (4.0 * UNIT)
            fold = 1.0 - jnp.abs(jnp.abs(y) - 1.0)
            s = coef * sine(jnp.where(y < 0, -fold, fold), 1.0)
            for i in range(2):
                xs[g * 2 + i, 0:4, at] = x[4 * i:4 * i + 4]
                srcs[g * 2 + i, 0:4, :] += s[4 * i:4 * i + 4]

    each(0, LANES // 128, points)

    def target(s, n):
        power = 1 + 3 * n + 9 * (n * (n - 1) // 2) + 27 * (n * (n - 1) * (n - 2) // 6)
        a, b = (sum((TREE[4 * s + i][0][d] % 4) * 4**i for i in range(4)) for d in range(2))
        return ((my + (b // power) % 4) % 4) * 4 + (mx + (a // power) % 4) % 4

    def noise(t):
        for p in range(4):
            here = pl.ds(p * 16, 16)
            seed = seed_ref[t, here, :]
            squares = None
            for l in range(LANES // 128):
                at = pl.ds(l * 128, 128)
                h0, h1 = hs[0, :, at], hs[1, :, at]
                h0 = jnp.concatenate([h0, h0], axis=0)
                h1 = jnp.concatenate([h1, h1], axis=0)
                u0 = ((rounds(h0 ^ seed) & LOW).astype(F32) + 0.5) * UNIT
                w = jnp.maximum(-2.0 * jnp.log(u0), 1e-9)
                r = w * lax.rsqrt(w)
                a = (rounds(h1 ^ seed) & LOW).astype(F32) + (0.5 - 4194304.0)
                y = (jnp.abs(a) - 2097152.0) * (4.0 * UNIT)
                e = r * sine(y, 2.0)
                z = jnp.broadcast_to(xs[t, p:p + 1, at], (16, 128)) + e
                q = e * e
                if l == LANES // 128 - 1:
                    z = jnp.where(tail_mask, z, 0.0)
                    q = jnp.where(tail_mask, q, 0.0)
                zs[t, here, at] = z.astype(BF16)
                squares = q if squares is None else squares + q
            sqs[t, here, :] = squares

    def first_layer(s, n):
        at = pl.ds(pl.multiple_of(n * 256, 256), 256)
        left = jnp.concatenate([zs[target(s, i)] for i in range(4)], axis=0)
        acc[:, at] = jnp.dot(left, w1s[:, at], preferred_element_type=F32)

    eye = jnp.where(
        lax.broadcasted_iota(I32, (ROWS, 128), 0) == lax.broadcasted_iota(I32, (ROWS, 128), 1), 1.0, 0.0
    )
    tail_mask = lax.broadcasted_iota(I32, (16, 128), 1) < WIDTH - 3072

    def stats_of(t):
        sq = jnp.sum(sqs[t], axis=1, keepdims=True)
        row_sq = jnp.sum(eye * sq, axis=0, keepdims=True)
        src = jnp.sum(srcs[t], axis=1, keepdims=True)
        row_src = jnp.sum(jnp.where(lane8 // 16 == row8, src, 0.0), axis=0, keepdims=True)
        return jnp.where(row8 == 0, row_sq, jnp.where(row8 == 1, row_src, 0.0))

    def toward(move):
        (dx, dy) = move
        return (pts, ((my + dy + 4) % 4) * 8 + zh * 4 + (mx + dx + 4) % 4)

    def partial_copy(n):
        return remote(psend.at[n], precv.at[n], p_ss.at[n], p_rs.at[n], toward(TREE[n][1]))

    def stat_copy(n):
        return remote(ssend.at[n], srecv.at[n], s_ss.at[n], s_rs.at[n], toward(TREE[n][1]))

    def gathered(n, i, t):
        value, tile = acc[i * ROWS:(i + 1) * ROWS, :], stats_of(t)
        for child in CHILDREN[n]:
            partial_copy(child).wait_recv()
            stat_copy(child).wait_recv()
            value += precv[child].astype(F32)
            tile += srecv[child]
        return value.astype(BF16), tile

    for s in range(5):
        if s == 1:
            loads[0].wait()
            loads[1].wait()

        def both(n, s=s):
            if s < 4:
                noise(target(s, n))
            if s > 0:
                first_layer(s - 1, n)

        each(0, 4, both)
        if s == 0:
            continue
        if s == 1:
            pl.semaphore_wait(barrier, XY - 1 + 5)
        ts = [target(s - 1, i) for i in range(4)]
        for i, t in enumerate(ts):
            n = 4 * s - 4 + i
            value, tile = gathered(n, i, t)
            if n < XY - 1:
                psend[n] = value
                ssend[n] = tile
                partial_copy(n).start()
                stat_copy(n).start()
            else:
                zsend[...] = value
                tsend[...] = tile

    z_copy = remote(zsend, zrecv, z_ss.at[0], z_rs.at[0], zpeer)
    t_copy = remote(tsend, trecv, z_ss.at[1], z_rs.at[1], zpeer)
    z_copy.start()
    t_copy.start()
    loads[2].wait()
    z_copy.wait_recv()
    t_copy.wait_recv()

    pre = (zsend[...].astype(F32) + zrecv[...].astype(F32)) + b1_ref[...]
    h1 = jnp.tanh(pre).astype(BF16)
    h1s[...] = h1
    two = jnp.tanh(
        lax.dot_general(h1, w2s[...], (((1,), (1,)), ((), ())), preferred_element_type=F32)
    ).astype(BF16)
    stat = tsend[...] + trecv[...]
    sq = jnp.sum(eye * stat[0:1, :], axis=1, keepdims=True) * 0.25
    src = jnp.sum(eye * stat[1:2, :], axis=1, keepdims=True) / math.sqrt(D)
    two_float = two.astype(F32)
    w3 = w3_ref[...].astype(F32)
    value = 0.0625 * jnp.sum(two_float * w3, axis=1, keepdims=True)
    stein = (sq - D) / 64.0
    prod = jnp.broadcast_to(stein * value, (ROWS, 128)).reshape(4, 16, 128)
    residual = jnp.broadcast_to(jnp.sum(prod, axis=1, keepdims=True), (4, 16, 128)).reshape(ROWS, 128) - src
    for n in range(2):
        @pl.when(zh == n)
        def _():
            first = lax.broadcasted_iota(I32, (1, 128), 1) == 0
            res_ref[0:1, :] = jnp.where(first, residual[32 * n:32 * n + 1, :], residual[32 * n + 16:32 * n + 17, :])

    dval = residual * stein
    dpre2 = (0.0625 * dval[:, 0:1] * w3 * (1.0 - two_float * two_float)).astype(BF16)
    back = jnp.dot(dpre2, w2s[...], preferred_element_type=F32)
    one_float = h1.astype(F32)
    dpre1 = (back * (1.0 - one_float * one_float)).astype(BF16)
    for j in range(4):
        part = dpre1[:, 256 * j:256 * j + 256]
        dbuf[j] = part
        dall[j, me] = part
        h2s[j] = two[:, 256 * j:256 * j + 256]
        d2s[j] = dpre2[:, 256 * j:256 * j + 256]

    def at_offset(o):
        return ((my + o[1] + 4) % 4) * 4 + (mx + o[0] + 4) % 4

    def origin(o):
        return ((my - o[1] + 4) % 4) * 4 + (mx - o[0] + 4) % 4

    def near_copy(j, k):
        return remote(dbuf.at[j], dall.at[j, me], a_ss.at[j * XY + k], a_rs.at[j * XY + me], plane(at_offset(NEAR[k])))

    def relay_copy(j, k):
        slot = origin(RELAY[k][0])
        return remote(
            dall.at[j, slot], dall.at[j, slot], a_ss.at[j * XY + 8 + k], a_rs.at[j * XY + slot], toward(RELAY[k][1]))

    def came(j, o):
        slot = origin(o)
        remote(dbuf.at[j], dall.at[j, slot], a_ss.at[j * XY], a_rs.at[j * XY + slot], plane(slot)).wait_recv()

    def pass_on(j):
        for o in PASSED:
            came(j, o)
            for k, (first, _) in enumerate(RELAY):
                if first == o:
                    relay_copy(j, k).start()

    inside, upper = zlo * (3 - zlo) // 2, zlo // 2

    def order(q):
        base = (1 - inside) * (3 - q) + inside * ((q % 2) * (q // 2) + (1 - q % 2) * (3 - q // 2))
        return upper * 3 + (1 - 2 * upper) * base

    def sends(q):
        for k in range(8):
            near_copy(order(q), k).start()

    each(0, 4, sends)

    lane64 = lax.broadcasted_iota(I32, (ROWS, 128), 1)
    high = dval.astype(BF16)
    low = (dval - high.astype(F32)).astype(BF16)
    zero = jnp.zeros_like(dval)
    pick0 = jnp.where(lane64 == 0, 1.0, zero).astype(BF16)
    pick1 = jnp.where(lane64 == 1, high.astype(F32), jnp.where(lane64 == 2, low.astype(F32), zero)).astype(BF16)
    rows_of = (((0,), (0,)), ((), ()))
    half = pl.ds(pl.multiple_of(zh * 128, 128), 128)
    for j in range(4):
        main = lax.dot_general(d2s[j, :, half], h1, rows_of, preferred_element_type=F32)
        more = lax.dot_general(dbuf[j, :, half], pick0, rows_of, preferred_element_type=F32)
        more += lax.dot_general(h2s[j, :, half], pick1, rows_of, preferred_element_type=F32)
        gbuf[j, :, 0:HID] = main.astype(BF16)
        gbuf[j, :, HID:WIDE] = more.astype(BF16)
    grecv[me] = gbuf[my, pl.ds(pl.multiple_of(mx * 32, 32), 32), :]

    def small_copy(t, slot):
        mine = gbuf.at[t // 4, pl.ds(pl.multiple_of((t % 4) * 32, 32), 32)]
        return remote(mine, grecv.at[slot], g_ss.at[t], g_rs.at[slot], plane(t))


    def core_copy(n):
        return remote(bsend.at[n], brecv.at[n], b_ss.at[n], b_rs.at[n], sibling)

    def right_copy(n):
        return remote(lsend.at[n], lrecv.at[n], l_ss.at[n], l_rs.at[n], chip(zlo + 1))

    def left_copy(n):
        return remote(rsend.at[n], rrecv.at[n], r_ss.at[n], r_rs.at[n], chip(zlo - 1))

    def chip_sum(n):
        core_copy(n).wait_recv()
        return own[n] + brecv[n].astype(F32)

    def go_right(t, b):
        n = t * NSUB + b
        tmp[...] = chip_sum((3 - t) * NSUB + b)

        @pl.when(zlo > 0)
        def _():
            remote(lsend.at[n], lrecv.at[n], l_ss.at[n], l_rs.at[n], chip(zlo - 1)).wait_recv()
            tmp[...] += lrecv[n].astype(F32)

        lsend[n] = tmp[...].astype(BF16)
        right_copy(n).start()

    def go_left(t, b):
        n = t * NSUB + b
        tmp[...] = chip_sum(n)

        @pl.when(zlo < 3)
        def _():
            remote(rsend.at[n], rrecv.at[n], r_ss.at[n], r_rs.at[n], chip(zlo + 1)).wait_recv()
            tmp[...] += rrecv[n].astype(F32)

        rsend[n] = tmp[...].astype(BF16)
        left_copy(n).start()

    def onward(n):
        r, l = n - LAG * upper, n - LAG * (1 - upper)

        @pl.when((r >= 0) & (r < (3 - zlo) * NSUB))
        def _():
            go_right(r // NSUB, r % NSUB)

        @pl.when((l >= 0) & (l < zlo * NSUB))
        def _():
            go_left(l // NSUB, l % NSUB)

    def chunk(j, after):
        for o in NEAR + FAR:
            if o not in PASSED:
                came(j, o)
        for n, c in enumerate((1 - core, core)):
            block = dall[j, :, :, pl.ds(pl.multiple_of(c * 128, 128), 128)].reshape(XY * ROWS, 128)
            dt[128 * n:128 * n + 128, :] = jnp.transpose(block)

        def sub(b):
            at = pl.ds(pl.multiple_of(b * SUB, 128), SUB)
            right = zs[:, :, at].reshape(XY * ROWS, SUB)
            part = jnp.dot(dt[...], right, preferred_element_type=F32)
            n = j * NSUB + b
            bsend[n] = part[0:128].astype(BF16)
            core_copy(n).start()
            own[n] = part[128:256]
            after(b)

        each(0, NSUB, sub)

    def columns(q):
        def after(b):
            @pl.when((inside == 0) & (q < 3) & (b >= 2))
            def _():
                onward(q * NSUB + b - 2)

        @pl.when(q < 3)
        def _():
            pass_on(order(q + 1))

        @pl.when(q == 2)
        def _():
            each(1, XY, lambda p: small_copy((me + p) % XY, me).start())

        chunk(order(q), after)
        lo = (1 - inside) * (q * NSUB + NSUB - 2)
        hi = (1 - inside) * (q * NSUB + NSUB) + inside * (q // 2) * (1 - q % 2) * (2 * NSUB + LAG)

        @pl.when(q < 3)
        def _():
            each(lo, hi, onward)

    pass_on(order(0))
    each(0, 4, columns)

    def small_there(p):
        slot = (me + p) % XY
        small_copy(slot, slot).wait_recv()

    each(1, XY, small_there)
    for r in range(2):
        at = slice(16 * r, 16 * r + 16)
        tot = grecv[0, at, :].astype(F32)
        for n in range(1, XY):
            tot += grecv[n, at, :].astype(F32)
        gtot[at, :] = tot
    theirs = pl.ds(pl.multiple_of(16 * (1 - core), 16), 16)
    mine = pl.ds(pl.multiple_of(16 * core, 16), 16)
    hsend[...] = gtot[theirs, :].astype(BF16)
    h_copy = remote(hsend, hrecv, h_ss.at[0], h_rs.at[0], sibling)
    h_copy.start()

    def across(z, slot):
        return remote(csend, crecv.at[slot], c_ss.at[z], c_rs.at[slot], chip(z))

    h_copy.wait_recv()
    total = (gtot[mine, :] + hrecv[...].astype(F32)).astype(BF16)
    csend[...] = total
    crecv[zlo] = total
    for p in (1, 2, 3):
        across((zlo + p) % 4, zlo).start()
    for p in (1, 2, 3):
        across((zlo + p) % 4, (zlo + p) % 4).wait_recv()
    total = crecv[0].astype(F32)
    for n in range(1, 4):
        total += crecv[n].astype(F32)
    fsend[...] = total
    gtot[mine, :] = total
    f_copy = remote(fsend, frecv, h_ss.at[1], h_rs.at[1], sibling)
    f_copy.start()
    f_copy.wait_recv()
    gtot[theirs, :] = frecv[...]
    g2_ref[...] = gtot[:, 0:HID]
    small = gtot[:, HID:WIDE]
    eye32 = eye[0:32, :]
    res_ref[2:3, :] = jnp.sum(eye32 * small[:, 0:1], axis=0, keepdims=True)
    res_ref[3:4, :] = 0.0625 * jnp.sum(eye32 * (small[:, 1:2] + small[:, 2:3]), axis=0, keepdims=True)

    def finish(b):
        tmp[...] = chip_sum(zlo * NSUB + b)

        @pl.when(zlo > 0)
        def _():
            n = (3 - zlo) * NSUB + b
            remote(lsend.at[n], lrecv.at[n], l_ss.at[n], l_rs.at[n], chip(zlo - 1)).wait_recv()
            tmp[...] += lrecv[n].astype(F32)

        @pl.when(zlo < 3)
        def _():
            n = zlo * NSUB + b
            remote(rsend.at[n], rrecv.at[n], r_ss.at[n], r_rs.at[n], chip(zlo + 1)).wait_recv()
            tmp[...] += rrecv[n].astype(F32)

        grad_ref[:, pl.ds(pl.multiple_of(b * SUB, 128), SUB)] = tmp[...].astype(BF16)

    each(0, NSUB, finish)

    def left_plane(p):
        t = (me + p) % XY
        small_copy(t, me).wait_send()

    each(1, XY, left_plane)

    def gather_left(j):
        for k in range(8):
            near_copy(j, k).wait_send()
        for k in range(7):
            relay_copy(j, k).wait_send()

    each(0, 4, gather_left)
    for n in range(XY - 1):
        partial_copy(n).wait_send()
        stat_copy(n).wait_send()
    z_copy.wait_send()
    t_copy.wait_send()
    h_copy.wait_send()
    f_copy.wait_send()
    for p in (1, 2, 3):
        across((zlo + p) % 4, zlo).wait_send()
    each(0, 4 * NSUB, lambda n: core_copy(n).wait_send())
    each(0, (3 - zlo) * NSUB, lambda n: right_copy(n).wait_send())
    each(0, zlo * NSUB, lambda n: left_copy(n).wait_send())


def shards(point_seed, pert_seed, source_coef, w1, b1, w2, w3):
    coef = jnp.pad(source_coef.reshape(1, WIDTH), ((0, 0), (0, LANES - WIDTH)))
    w1t = w1.T
    tail = jnp.pad(w1t[3072:], ((0, LANES - WIDTH), (0, 0)))
    vmem = pl.BlockSpec(memory_space=pltpu.VMEM)
    anyw = pl.BlockSpec(memory_space=pl.ANY)
    dma = lambda n: pltpu.SemaphoreType.DMA((n,))
    v = pltpu.VMEM
    n15, n20 = 3 * NSUB, 4 * NSUB
    residual, grad, small = pl.pallas_call(
        kernel,
        name="pinn_step",
        out_shape=(
            jax.ShapeDtypeStruct((8, 128), F32),
            jax.ShapeDtypeStruct((128, LANES), BF16),
            jax.ShapeDtypeStruct((32, HID), F32),
        ),
        in_specs=[vmem, vmem, vmem, anyw, anyw, vmem, anyw, vmem],
        out_specs=(vmem, vmem, vmem),
        scratch_shapes=[
            v((XY, ROWS, 128), I32), v((64, 128), I32), v((LANES, HID), BF16), v((HID, HID), BF16), v((XY, ROWS, LANES), BF16),
            v((XY, 8, LANES), F32), v((2, 8, LANES), I32), v((XY, ROWS, 128), F32), v((XY, 8, 128), F32),
            v((256, HID), F32),
            v((XY, ROWS, HID), BF16), v((XY, ROWS, HID), BF16), v((XY, 8, 128), F32), v((XY, 8, 128), F32),
            v((ROWS, HID), BF16), v((ROWS, HID), BF16), v((8, 128), F32), v((8, 128), F32),
            v((ROWS, HID), BF16), v((4, ROWS, 256), BF16), v((4, ROWS, 256), BF16), v((4, ROWS, 256), BF16),
            v((4, XY, ROWS, 256), BF16), v((256, XY * ROWS), BF16),
            v((n20, 128, SUB), F32), v((n20, 128, SUB), BF16), v((n20, 128, SUB), BF16), v((128, SUB), F32),
            v((n15, 128, SUB), BF16), v((n15, 128, SUB), BF16), v((n15, 128, SUB), BF16), v((n15, 128, SUB), BF16),
            v((4, 128, WIDE), BF16), v((XY, 32, WIDE), BF16), v((32, WIDE), F32),
            v((16, WIDE), BF16), v((16, WIDE), BF16), v((16, WIDE), BF16), v((4, 16, WIDE), BF16),
            v((16, WIDE), F32), v((16, WIDE), F32),
            dma(3), dma(XY), dma(XY), dma(XY), dma(XY), dma(2), dma(2), dma(4 * XY), dma(4 * XY), dma(n20), dma(n20),
            dma(n15), dma(n15), dma(n15), dma(n15), dma(XY), dma(XY), dma(2), dma(2), dma(4), dma(4),
        ],
        compiler_params=pltpu.CompilerParams(
            collective_id=0, has_side_effects=True, vmem_limit_bytes=66_000_000
        ),
    )(pert_seed.T, point_seed.reshape(1, 64), coef, w1t, tail, b1.reshape(1, HID), w2, w3.reshape(1, HID))
    return residual[0, 0:2], grad[:, :WIDTH], small, residual[2, 0:32], residual[3, 0:32]


def solution(mesh):
    return jax.shard_map(
        shards,
        mesh=mesh,
        in_specs=(P("pts"), P("pts", None), P("coord"), P(None, "coord"), P(), P(), P()),
        out_specs=(
            P(("pts", "coord")),
            P("pts", "coord"),
            P("coord", None),
            P("coord"),
            P("coord"),
        ),
        check_vma=False,
    )
```

```python
import math

import jax
import jax.numpy as jnp
from jax import lax
from jax.experimental import pallas as pl
from jax.experimental.pallas import tpu as pltpu
from jax.sharding import PartitionSpec as P

D = 100000
HASH = 73244475
MESH = pl.DeviceIdType.MESH
F32, BF16, I32 = jnp.float32, jnp.bfloat16, jnp.int32
SINE = (1.5707962900223675, -0.6459633598658464, 0.07968848054018324, -0.004672227923047835, 0.00015082056445751214)
LOW = 8388607
UNIT = 1.0 / 8388608.0

XY = 16
ROWS = 64
HID = 1024
WIDTH = 3125
LANES = 3200
SUB = 640
NSUB = LANES // SUB
LAG = 2
KC = 256
WIDE = HID + 128

TREE = (
    ((2, 2), (1, 0)), ((2, 1), (0, 1)), ((2, -1), (-1, 0)), ((-1, 2), (0, -1)),
    ((1, 2), (0, 1)), ((2, 0), (1, 0)), ((0, 2), (0, -1)), ((-1, -1), (-1, 0)),
    ((1, 1), (1, 0)), ((-1, 1), (0, 1)), ((1, -1), (0, -1)), ((0, -1), (0, -1)),
    ((1, 0), (1, 0)), ((-1, 0), (-1, 0)), ((0, 1), (0, 1)), ((0, 0), None),
)


NEAR = ((1, 1), (-1, -1), (1, 0), (0, 1), (-1, 1), (1, -1), (-1, 0), (0, -1))
RELAY = (((1, 1), (1, 1)), ((1, 1), (0, 1)), ((1, 0), (1, 0)), ((0, 1), (0, 1)), ((-1, -1), (-1, 0)), ((-1, -1), (0, -1)), ((-1, 1), (-1, 0)))
PASSED = tuple(dict.fromkeys(o for o, _ in RELAY))
FAR = tuple(((o[0] + m[0] + 1) % 4 - 1, (o[1] + m[1] + 1) % 4 - 1) for o, m in RELAY)
assert len(set(NEAR + FAR)) == XY - 1 and (0, 0) not in NEAR + FAR


def lands(n):
    (a, b), move = TREE[n]
    if move is None:
        return None
    return tuple((v + 1) % 4 - 1 for v in (a - move[0], b - move[1]))


CHILDREN = [[m for m in range(XY) if lands(m) == TREE[n][0]] for n in range(XY)]
assert all(m // 4 < n // 4 for n in range(XY - 1) for m in CHILDREN[n])


def shuffle_bits(v):
    return v ^ lax.shift_right_logical(v, jnp.full_like(v, 16))


def rounds(v):
    v = shuffle_bits(v * HASH)
    return shuffle_bits(v * HASH)


def sine(y, scale):
    t = y * y
    acc = t * (SINE[4] * scale) + (SINE[3] * scale)
    for c in (SINE[2], SINE[1], SINE[0]):
        acc = acc * t + (c * scale)
    return acc * y


def kernel(
    pert_ref, point_ref, coef_ref, w1_ref, w1t_ref, b1_ref, w2_ref, w3_ref,
    res_ref, grad_ref, g2_ref,
    seed_ref, pseed_ref, coefs, w1s, w2s, zs, xs, hs, sqs, srcs, acc,
    psend, precv, ssend, srecv, zsend, zrecv, tsend, trecv,
    h1s, h2s, d2s, dbuf, dall, dt, own, bsend, brecv, tmp, lsend, lrecv, rsend, rrecv,
    gbuf, grecv, gtot, hsend, hrecv, csend, crecv, fsend, frecv,
    load_sem, p_ss, p_rs, s_ss, s_rs, z_ss, z_rs, a_ss, a_rs, b_ss, b_rs,
    l_ss, l_rs, r_ss, r_rs, g_ss, g_rs, h_ss, h_rs, c_ss, c_rs,
):
    pts, coord = lax.axis_index("pts"), lax.axis_index("coord")
    zlo, core = pts // 2, pts % 2
    mx, zh, my = coord % 4, (coord // 4) % 2, coord // 8
    me = my * 4 + mx

    def plane(t):
        return (pts, (t // 4) * 8 + zh * 4 + t % 4)

    zpeer = (pts, coord + 4 - 8 * zh)
    sibling = (pts + 1 - 2 * core, coord)

    def chip(z):
        return (z * 2 + core, coord)

    def remote(src, dst, ss, rs, device):
        return pltpu.make_async_remote_copy(src, dst, ss, rs, device_id=device, device_id_type=MESH)

    def each(lo, hi, body):
        def run(i, c):
            body(i)
            return c

        lax.fori_loop(lo, hi, run, 0)

    loads = [
        pltpu.make_async_copy(w1_ref.at[pl.ds(0, 3072)], w1s.at[pl.ds(0, 3072)], load_sem.at[0]),
        pltpu.make_async_copy(w1_ref.at[pl.ds(3072, 48)], w1s.at[pl.ds(3072, 48)], load_sem.at[1]),
        pltpu.make_async_copy(w2_ref, w2s, load_sem.at[2]),
    ]
    for c in loads:
        c.start()
    w1s[3120:LANES, :] = jnp.zeros((LANES - 3120, HID), BF16)
    w1s[3120:WIDTH, :] = w1t_ref[...]
    barrier = pltpu.get_barrier_semaphore()

    def greet(device):
        pl.semaphore_signal(barrier, inc=1, device_id=device, device_id_type=MESH)

    each(1, XY, lambda p: greet(plane((me + p) % XY)))
    greet(zpeer)
    greet(sibling)
    for p in (1, 2, 3):
        greet(chip((zlo + p) % 4))

    for n in range(64):
        pos = ((n // 16) * 4 + (n // 2) % 4, ((n // 8) % 2) * 2 + n % 2)
        seed = jnp.broadcast_to(pert_ref[:, n:n + 1], (16, 128))
        seed_ref[pos[0], 16 * pos[1]:16 * pos[1] + 16, :] = shuffle_bits(seed)
    r64 = lax.broadcasted_iota(I32, (64, 64), 0)
    place = (((r64 // 16) * 2 + (r64 // 2) % 2) * 4 + (r64 // 4) % 4) * 2 + r64 % 2
    spread = jnp.where(place == lax.broadcasted_iota(I32, (64, 64), 1), point_ref[...].astype(F32), 0.0)
    spread = jnp.sum(spread, axis=1, keepdims=True).astype(I32)
    pseed_ref[...] = shuffle_bits(jnp.broadcast_to(spread, (64, 128)))

    srcs[...] = jnp.zeros_like(srcs)
    coefs[...] = jnp.zeros_like(coefs)
    coefs[:, 0:WIDTH] = coef_ref[...]
    lane8 = lax.broadcasted_iota(I32, (8, 128), 1)
    row8 = lax.broadcasted_iota(I32, (8, 128), 0)

    def points(k):
        at = pl.ds(pl.multiple_of(k * 128, 128), 128)
        col = (coord * WIDTH + k * 128 + lane8) * 4
        for n in range(3):
            h = rounds(shuffle_bits(col + n))
            if n < 2:
                hs[n, :, at] = shuffle_bits(h)
        h = shuffle_bits(h)
        coef = jnp.broadcast_to(coefs[:, at], (8, 128))
        for g in range(8):
            v = rounds(h ^ pseed_ref[8 * g:8 * g + 8, :])
            t = (v & LOW).astype(F32) + (0.5 - 4194304.0)
            x = t * (2.0 * UNIT)
            y = t * (4.0 * UNIT)
            fold = 1.0 - jnp.abs(jnp.abs(y) - 1.0)
            s = coef * sine(jnp.where(y < 0, -fold, fold), 1.0)
            for i in range(2):
                xs[g * 2 + i, 0:4, at] = x[4 * i:4 * i + 4]
                srcs[g * 2 + i, 0:4, :] += s[4 * i:4 * i + 4]

    each(0, LANES // 128, points)

    def target(s, n):
        power = 1 + 3 * n + 9 * (n * (n - 1) // 2) + 27 * (n * (n - 1) * (n - 2) // 6)
        a, b = (sum((TREE[4 * s + i][0][d] % 4) * 4**i for i in range(4)) for d in range(2))
        return ((my + (b // power) % 4) % 4) * 4 + (mx + (a // power) % 4) % 4

    def noise(t):
        for p in range(4):
            here = pl.ds(p * 16, 16)
            seed = seed_ref[t, here, :]
            squares = None
            for l in range(LANES // 128):
                at = pl.ds(l * 128, 128)
                h0, h1 = hs[0, :, at], hs[1, :, at]
                h0 = jnp.concatenate([h0, h0], axis=0)
                h1 = jnp.concatenate([h1, h1], axis=0)
                u0 = ((rounds(h0 ^ seed) & LOW).astype(F32) + 0.5) * UNIT
                w = jnp.maximum(-2.0 * jnp.log(u0), 1e-9)
                r = w * lax.rsqrt(w)
                a = (rounds(h1 ^ seed) & LOW).astype(F32) + (0.5 - 4194304.0)
                y = (jnp.abs(a) - 2097152.0) * (4.0 * UNIT)
                e = r * sine(y, 2.0)
                z = jnp.broadcast_to(xs[t, p:p + 1, at], (16, 128)) + e
                q = e * e
                if l == LANES // 128 - 1:
                    z = jnp.where(tail_mask, z, 0.0)
                    q = jnp.where(tail_mask, q, 0.0)
                zs[t, here, at] = z.astype(BF16)
                squares = q if squares is None else squares + q
            sqs[t, here, :] = squares

    def first_layer(s, n):
        at = pl.ds(pl.multiple_of(n * 256, 256), 256)
        left = jnp.concatenate([zs[target(s, i)] for i in range(4)], axis=0)
        acc[:, at] = jnp.dot(left, w1s[:, at], preferred_element_type=F32)

    eye = jnp.where(
        lax.broadcasted_iota(I32, (ROWS, 128), 0) == lax.broadcasted_iota(I32, (ROWS, 128), 1), 1.0, 0.0
    )
    tail_mask = lax.broadcasted_iota(I32, (16, 128), 1) < WIDTH - 3072

    def stats_of(t):
        sq = jnp.sum(sqs[t], axis=1, keepdims=True)
        row_sq = jnp.sum(eye * sq, axis=0, keepdims=True)
        src = jnp.sum(srcs[t], axis=1, keepdims=True)
        row_src = jnp.sum(jnp.where(lane8 // 16 == row8, src, 0.0), axis=0, keepdims=True)
        return jnp.where(row8 == 0, row_sq, jnp.where(row8 == 1, row_src, 0.0))

    def toward(move):
        (dx, dy) = move
        return (pts, ((my + dy + 4) % 4) * 8 + zh * 4 + (mx + dx + 4) % 4)

    def partial_copy(n):
        return remote(psend.at[n], precv.at[n], p_ss.at[n], p_rs.at[n], toward(TREE[n][1]))

    def stat_copy(n):
        return remote(ssend.at[n], srecv.at[n], s_ss.at[n], s_rs.at[n], toward(TREE[n][1]))

    def gathered(n, i, t):
        value, tile = acc[i * ROWS:(i + 1) * ROWS, :], stats_of(t)
        for child in CHILDREN[n]:
            partial_copy(child).wait_recv()
            stat_copy(child).wait_recv()
            value += precv[child].astype(F32)
            tile += srecv[child]
        return value.astype(BF16), tile

    for s in range(5):
        if s == 1:
            loads[0].wait()
            loads[1].wait()

        def both(n, s=s):
            if s < 4:
                noise(target(s, n))
            if s > 0:
                first_layer(s - 1, n)

        each(0, 4, both)
        if s == 0:
            continue
        if s == 1:
            pl.semaphore_wait(barrier, XY - 1 + 5)
        ts = [target(s - 1, i) for i in range(4)]
        for i, t in enumerate(ts):
            n = 4 * s - 4 + i
            value, tile = gathered(n, i, t)
            if n < XY - 1:
                psend[n] = value
                ssend[n] = tile
                partial_copy(n).start()
                stat_copy(n).start()
            else:
                zsend[...] = value
                tsend[...] = tile

    z_copy = remote(zsend, zrecv, z_ss.at[0], z_rs.at[0], zpeer)
    t_copy = remote(tsend, trecv, z_ss.at[1], z_rs.at[1], zpeer)
    z_copy.start()
    t_copy.start()
    loads[2].wait()
    z_copy.wait_recv()
    t_copy.wait_recv()

    pre = (zsend[...].astype(F32) + zrecv[...].astype(F32)) + b1_ref[...]
    h1 = jnp.tanh(pre).astype(BF16)
    h1s[...] = h1
    two = jnp.tanh(
        lax.dot_general(h1, w2s[...], (((1,), (1,)), ((), ())), preferred_element_type=F32)
    ).astype(BF16)
    stat = tsend[...] + trecv[...]
    sq = jnp.sum(eye * stat[0:1, :], axis=1, keepdims=True) * 0.25
    src = jnp.sum(eye * stat[1:2, :], axis=1, keepdims=True) / math.sqrt(D)
    two_float = two.astype(F32)
    w3 = w3_ref[...].astype(F32)
    value = 0.0625 * jnp.sum(two_float * w3, axis=1, keepdims=True)
    stein = (sq - D) / 64.0
    prod = jnp.broadcast_to(stein * value, (ROWS, 128)).reshape(4, 16, 128)
    residual = jnp.broadcast_to(jnp.sum(prod, axis=1, keepdims=True), (4, 16, 128)).reshape(ROWS, 128) - src
    for n in range(2):
        @pl.when(zh == n)
        def _():
            first = lax.broadcasted_iota(I32, (1, 128), 1) == 0
            res_ref[0:1, :] = jnp.where(first, residual[32 * n:32 * n + 1, :], residual[32 * n + 16:32 * n + 17, :])

    dval = residual * stein
    dpre2 = (0.0625 * dval[:, 0:1] * w3 * (1.0 - two_float * two_float)).astype(BF16)
    back = jnp.dot(dpre2, w2s[...], preferred_element_type=F32)
    one_float = h1.astype(F32)
    dpre1 = (back * (1.0 - one_float * one_float)).astype(BF16)
    for j in range(4):
        part = dpre1[:, 256 * j:256 * j + 256]
        dbuf[j] = part
        dall[j, me] = part
        h2s[j] = two[:, 256 * j:256 * j + 256]
        d2s[j] = dpre2[:, 256 * j:256 * j + 256]

    def at_offset(o):
        return ((my + o[1] + 4) % 4) * 4 + (mx + o[0] + 4) % 4

    def origin(o):
        return ((my - o[1] + 4) % 4) * 4 + (mx - o[0] + 4) % 4

    def near_copy(j, k):
        return remote(dbuf.at[j], dall.at[j, me], a_ss.at[j * XY + k], a_rs.at[j * XY + me], plane(at_offset(NEAR[k])))

    def relay_copy(j, k):
        slot = origin(RELAY[k][0])
        return remote(
            dall.at[j, slot], dall.at[j, slot], a_ss.at[j * XY + 8 + k], a_rs.at[j * XY + slot], toward(RELAY[k][1]))

    def came(j, o):
        slot = origin(o)
        remote(dbuf.at[j], dall.at[j, slot], a_ss.at[j * XY], a_rs.at[j * XY + slot], plane(slot)).wait_recv()

    def pass_on(j):
        for o in PASSED:
            came(j, o)
            for k, (first, _) in enumerate(RELAY):
                if first == o:
                    relay_copy(j, k).start()

    inside, upper = zlo * (3 - zlo) // 2, zlo // 2

    def order(q):
        base = (1 - inside) * (3 - q) + inside * ((q % 2) * (q // 2) + (1 - q % 2) * (3 - q // 2))
        return upper * 3 + (1 - 2 * upper) * base

    def sends(q):
        for k in range(8):
            near_copy(order(q), k).start()

    each(0, 4, sends)

    lane64 = lax.broadcasted_iota(I32, (ROWS, 128), 1)
    high = dval.astype(BF16)
    low = (dval - high.astype(F32)).astype(BF16)
    zero = jnp.zeros_like(dval)
    pick0 = jnp.where(lane64 == 0, 1.0, zero).astype(BF16)
    pick1 = jnp.where(lane64 == 1, high.astype(F32), jnp.where(lane64 == 2, low.astype(F32), zero)).astype(BF16)
    rows_of = (((0,), (0,)), ((), ()))
    half = pl.ds(pl.multiple_of(zh * 128, 128), 128)
    for j in range(4):
        main = lax.dot_general(d2s[j, :, half], h1, rows_of, preferred_element_type=F32)
        more = lax.dot_general(dbuf[j, :, half], pick0, rows_of, preferred_element_type=F32)
        more += lax.dot_general(h2s[j, :, half], pick1, rows_of, preferred_element_type=F32)
        gbuf[j, :, 0:HID] = main.astype(BF16)
        gbuf[j, :, HID:WIDE] = more.astype(BF16)
    grecv[me] = gbuf[my, pl.ds(pl.multiple_of(mx * 32, 32), 32), :]

    def small_copy(t, slot):
        mine = gbuf.at[t // 4, pl.ds(pl.multiple_of((t % 4) * 32, 32), 32)]
        return remote(mine, grecv.at[slot], g_ss.at[t], g_rs.at[slot], plane(t))


    def core_copy(n):
        return remote(bsend.at[n], brecv.at[n], b_ss.at[n], b_rs.at[n], sibling)

    def right_copy(n):
        return remote(lsend.at[n], lrecv.at[n], l_ss.at[n], l_rs.at[n], chip(zlo + 1))

    def left_copy(n):
        return remote(rsend.at[n], rrecv.at[n], r_ss.at[n], r_rs.at[n], chip(zlo - 1))

    def chip_sum(n):
        core_copy(n).wait_recv()
        return own[n] + brecv[n].astype(F32)

    def go_right(t, b):
        n = t * NSUB + b
        tmp[...] = chip_sum((3 - t) * NSUB + b)

        @pl.when(zlo > 0)
        def _():
            remote(lsend.at[n], lrecv.at[n], l_ss.at[n], l_rs.at[n], chip(zlo - 1)).wait_recv()
            tmp[...] += lrecv[n].astype(F32)

        lsend[n] = tmp[...].astype(BF16)
        right_copy(n).start()

    def go_left(t, b):
        n = t * NSUB + b
        tmp[...] = chip_sum(n)

        @pl.when(zlo < 3)
        def _():
            remote(rsend.at[n], rrecv.at[n], r_ss.at[n], r_rs.at[n], chip(zlo + 1)).wait_recv()
            tmp[...] += rrecv[n].astype(F32)

        rsend[n] = tmp[...].astype(BF16)
        left_copy(n).start()

    def onward(n):
        r, l = n - LAG * upper, n - LAG * (1 - upper)

        @pl.when((r >= 0) & (r < (3 - zlo) * NSUB))
        def _():
            go_right(r // NSUB, r % NSUB)

        @pl.when((l >= 0) & (l < zlo * NSUB))
        def _():
            go_left(l // NSUB, l % NSUB)

    def chunk(j, after):
        for o in NEAR + FAR:
            if o not in PASSED:
                came(j, o)
        for n, c in enumerate((1 - core, core)):
            block = dall[j, :, :, pl.ds(pl.multiple_of(c * 128, 128), 128)].reshape(XY * ROWS, 128)
            dt[128 * n:128 * n + 128, :] = jnp.transpose(block)

        def sub(b):
            at = pl.ds(pl.multiple_of(b * SUB, 128), SUB)
            right = zs[:, :, at].reshape(XY * ROWS, SUB)
            part = jnp.dot(dt[...], right, preferred_element_type=F32)
            n = j * NSUB + b
            bsend[n] = part[0:128].astype(BF16)
            core_copy(n).start()
            own[n] = part[128:256]
            after(b)

        each(0, NSUB, sub)

    def columns(q):
        def after(b):
            @pl.when((inside == 0) & (q < 3) & (b >= 2))
            def _():
                onward(q * NSUB + b - 2)

        @pl.when(q < 3)
        def _():
            pass_on(order(q + 1))

        @pl.when(q == 2)
        def _():
            each(1, XY, lambda p: small_copy((me + p) % XY, me).start())

        chunk(order(q), after)
        lo = (1 - inside) * (q * NSUB + NSUB - 2)
        hi = (1 - inside) * (q * NSUB + NSUB) + inside * (q // 2) * (1 - q % 2) * (2 * NSUB + LAG)

        @pl.when(q < 3)
        def _():
            each(lo, hi, onward)

    pass_on(order(0))
    each(0, 4, columns)

    def small_there(p):
        slot = (me + p) % XY
        small_copy(slot, slot).wait_recv()

    each(1, XY, small_there)
    for r in range(2):
        at = slice(16 * r, 16 * r + 16)
        tot = grecv[0, at, :].astype(F32)
        for n in range(1, XY):
            tot += grecv[n, at, :].astype(F32)
        gtot[at, :] = tot
    theirs = pl.ds(pl.multiple_of(16 * (1 - core), 16), 16)
    mine = pl.ds(pl.multiple_of(16 * core, 16), 16)
    hsend[...] = gtot[theirs, :].astype(BF16)
    h_copy = remote(hsend, hrecv, h_ss.at[0], h_rs.at[0], sibling)
    h_copy.start()

    def across(z, slot):
        return remote(csend, crecv.at[slot], c_ss.at[z], c_rs.at[slot], chip(z))

    h_copy.wait_recv()
    total = (gtot[mine, :] + hrecv[...].astype(F32)).astype(BF16)
    csend[...] = total
    crecv[zlo] = total
    for p in (1, 2, 3):
        across((zlo + p) % 4, zlo).start()
    for p in (1, 2, 3):
        across((zlo + p) % 4, (zlo + p) % 4).wait_recv()
    total = crecv[0].astype(F32)
    for n in range(1, 4):
        total += crecv[n].astype(F32)
    fsend[...] = total
    gtot[mine, :] = total
    f_copy = remote(fsend, frecv, h_ss.at[1], h_rs.at[1], sibling)
    f_copy.start()
    f_copy.wait_recv()
    gtot[theirs, :] = frecv[...]
    g2_ref[...] = gtot[:, 0:HID]
    small = gtot[:, HID:WIDE]
    eye32 = eye[0:32, :]
    res_ref[2:3, :] = jnp.sum(eye32 * small[:, 0:1], axis=0, keepdims=True)
    res_ref[3:4, :] = 0.0625 * jnp.sum(eye32 * (small[:, 1:2] + small[:, 2:3]), axis=0, keepdims=True)

    def finish(b):
        tmp[...] = chip_sum(zlo * NSUB + b)

        @pl.when(zlo > 0)
        def _():
            n = (3 - zlo) * NSUB + b
            remote(lsend.at[n], lrecv.at[n], l_ss.at[n], l_rs.at[n], chip(zlo - 1)).wait_recv()
            tmp[...] += lrecv[n].astype(F32)

        @pl.when(zlo < 3)
        def _():
            n = zlo * NSUB + b
            remote(rsend.at[n], rrecv.at[n], r_ss.at[n], r_rs.at[n], chip(zlo + 1)).wait_recv()
            tmp[...] += rrecv[n].astype(F32)

        grad_ref[:, pl.ds(pl.multiple_of(b * SUB, 128), SUB)] = tmp[...].astype(BF16)

    each(0, NSUB, finish)

    def left_plane(p):
        t = (me + p) % XY
        small_copy(t, me).wait_send()

    each(1, XY, left_plane)

    def gather_left(j):
        for k in range(8):
            near_copy(j, k).wait_send()
        for k in range(7):
            relay_copy(j, k).wait_send()

    each(0, 4, gather_left)
    for n in range(XY - 1):
        partial_copy(n).wait_send()
        stat_copy(n).wait_send()
    z_copy.wait_send()
    t_copy.wait_send()
    h_copy.wait_send()
    f_copy.wait_send()
    for p in (1, 2, 3):
        across((zlo + p) % 4, zlo).wait_send()
    each(0, 4 * NSUB, lambda n: core_copy(n).wait_send())
    each(0, (3 - zlo) * NSUB, lambda n: right_copy(n).wait_send())
    each(0, zlo * NSUB, lambda n: left_copy(n).wait_send())


def shards(point_seed, pert_seed, source_coef, w1, b1, w2, w3):
    coef = source_coef.reshape(1, WIDTH)
    w1t = w1.T
    tail = w1t[3120:]
    vmem = pl.BlockSpec(memory_space=pltpu.VMEM)
    anyw = pl.BlockSpec(memory_space=pl.ANY)
    dma = lambda n: pltpu.SemaphoreType.DMA((n,))
    v = pltpu.VMEM
    n15, n20 = 3 * NSUB, 4 * NSUB
    residual, grad, small = pl.pallas_call(
        kernel,
        name="pinn_step",
        out_shape=(
            jax.ShapeDtypeStruct((8, 128), F32),
            jax.ShapeDtypeStruct((128, LANES), BF16),
            jax.ShapeDtypeStruct((32, HID), F32),
        ),
        in_specs=[vmem, vmem, vmem, anyw, vmem, vmem, anyw, vmem],
        out_specs=(vmem, vmem, vmem),
        scratch_shapes=[
            v((XY, ROWS, 128), I32), v((64, 128), I32), v((1, LANES), F32), v((LANES, HID), BF16), v((HID, HID), BF16), v((XY, ROWS, LANES), BF16),
            v((XY, 8, LANES), F32), v((2, 8, LANES), I32), v((XY, ROWS, 128), F32), v((XY, 8, 128), F32),
            v((256, HID), F32),
            v((XY, ROWS, HID), BF16), v((XY, ROWS, HID), BF16), v((XY, 8, 128), F32), v((XY, 8, 128), F32),
            v((ROWS, HID), BF16), v((ROWS, HID), BF16), v((8, 128), F32), v((8, 128), F32),
            v((ROWS, HID), BF16), v((4, ROWS, 256), BF16), v((4, ROWS, 256), BF16), v((4, ROWS, 256), BF16),
            v((4, XY, ROWS, 256), BF16), v((256, XY * ROWS), BF16),
            v((n20, 128, SUB), F32), v((n20, 128, SUB), BF16), v((n20, 128, SUB), BF16), v((128, SUB), F32),
            v((n15, 128, SUB), BF16), v((n15, 128, SUB), BF16), v((n15, 128, SUB), BF16), v((n15, 128, SUB), BF16),
            v((4, 128, WIDE), BF16), v((XY, 32, WIDE), BF16), v((32, WIDE), F32),
            v((16, WIDE), BF16), v((16, WIDE), BF16), v((16, WIDE), BF16), v((4, 16, WIDE), BF16),
            v((16, WIDE), F32), v((16, WIDE), F32),
            dma(3), dma(XY), dma(XY), dma(XY), dma(XY), dma(2), dma(2), dma(4 * XY), dma(4 * XY), dma(n20), dma(n20),
            dma(n15), dma(n15), dma(n15), dma(n15), dma(XY), dma(XY), dma(2), dma(2), dma(4), dma(4),
        ],
        compiler_params=pltpu.CompilerParams(
            collective_id=0, has_side_effects=True, vmem_limit_bytes=66_000_000
        ),
    )(pert_seed.T, point_seed.reshape(1, 64), coef, w1t, tail, b1.reshape(1, HID), w2, w3.reshape(1, HID))
    return residual[0, 0:2], grad[:, :WIDTH], small, residual[2, 0:32], residual[3, 0:32]


def solution(mesh):
    return jax.shard_map(
        shards,
        mesh=mesh,
        in_specs=(P("pts"), P("pts", None), P("coord"), P(None, "coord"), P(), P(), P()),
        out_specs=(
            P(("pts", "coord")),
            P("pts", "coord"),
            P("coord", None),
            P("coord"),
            P("coord"),
        ),
        check_vma=False,
    )
```
